32 devices in a mesh: row: 16 (over z, y, core), col: 2 (over x).
Axes of the slice: x: 2, y: 2, z: 4, core: 2. Of those that a mesh axis runs over, the one named last changes fastest.
Arguments:
- row_embed: bfloat16 [300, 16384], P(None, 'row'), may hold values from -1.796875 to 1.796875
- col_embed: bfloat16 [300, 2, 256], P(None, 'col', 'row'), may hold values from -1.796875 to 1.796875
- counts: int32 [16384, 2, 256], P('row', 'col'), may hold values from 0 to 64, as said below
- occupancy: int32 [128, 2, 2], P('row', 'col'), may hold values from 0 to 1, as said below
- row_marg: int32 [16384], P('row'), may hold values from 2000 to 199999
- col_marg: int32 [2, 256], P('col', 'row'), may hold values from 2000 to 199999
- log_total: float32 [1], replicated, may hold values from 18 to 22
Outputs:
- grad_rows: float32 [300, 16384], P(None, 'row')
- grad_cols: float32 [300, 2, 256], P(None, 'col', 'row')
The draws below stay inside these ranges and needn't reach their ends.
Inputs may be any that keep to these rules, and one draw needn't show every extreme that they name: counts of the band's cells; zero in part of the cells. `occupancy`: the share of tiles marked 1 differs from row tile to row tile.
All inputs are finite; a program needn't handle non-finite values.
Results may differ from the reference program's by a relative error of at most 0.0018.
Values may be sent and summed in bfloat16 or wider, within the bound.
A program may use at most 64 MiB of HBM per device.

```python
import math
import jax
import jax.numpy as jnp
from jax import lax

D = 300
TILE = 128
ROW_DEV = 1024
ROWS = 16384
BAND = 256
BANDS = 2
COLS = 512
ROW_TILES = 128
BAND_TILES = 2


def draw_counts(key, part):
    present = jax.random.randint(jax.random.fold_in(key, 11), (ROWS, BANDS, BAND), 0, 2)
    values = jax.random.randint(jax.random.fold_in(key, 12), (ROWS, BANDS, BAND), 1, 65)
    result = (present * values).astype(jnp.int32)
    return result.at[0, 0, 0].set(64)


def draw_occupancy(key, part):
    levels = jax.random.randint(jax.random.fold_in(key, 21), (ROW_TILES, 1, 1), 1, 9)
    rolls = jax.random.randint(jax.random.fold_in(key, 22), (ROW_TILES, BANDS, BAND_TILES), 0, 8)
    return (rolls < levels).astype(jnp.int32)


def with_ends(values, rng, smallest, high):
    longest = values.shape.index(max(values.shape))
    spots = []
    for shift in (0, 1):
        where = [jax.random.randint(jax.random.fold_in(rng, axis), (), 0, length) for axis, length in enumerate(values.shape)]
        where[longest] = (where[longest] + shift) % values.shape[longest]
        spots.append(tuple(where))
    return values.at[spots[0]].set(smallest).at[spots[1]].set(high)


def block_scale(own_key, extent, shards, smallest, high):
    gain = 1.0
    for axis_at, blocks in shards:
        draws = jax.random.uniform(jax.random.fold_in(jax.random.fold_in(own_key, 6), axis_at), (blocks,), jnp.float32, smallest / len(shards), high / len(shards))
        gain = gain * jnp.repeat(jnp.exp(draws), extent[axis_at] // blocks).reshape((-1,) + (1,) * (len(extent) - 1 - axis_at))
    return gain


def normal_values(stream_key, extent, spread, most, shards=(), held_as=jnp.bfloat16):
    values = spread * jax.random.normal(stream_key, extent, jnp.float32)
    if shards:
        values = values * block_scale(stream_key, extent, shards, -0.22, 0.18)
    return jnp.clip(values, -most, most).astype(held_as)


def setup_inputs(seed: int = 0) -> dict:
    seeds = jax.random.split(jax.random.key(seed), 8)
    return {
        "row_embed": normal_values(seeds[0], (D, ROWS), 0.3, 1.796875, ((1, 16),)),
        "col_embed": normal_values(seeds[1], (D, BANDS, BAND), 0.3, 1.796875, ((1, 2), (2, 16))),
        "counts": draw_counts(jax.random.fold_in(seeds[7], 71), 0),
        "occupancy": draw_occupancy(jax.random.fold_in(seeds[7], 71), 0),
        "row_marg": with_ends(jax.random.randint(seeds[4], (ROWS,), 2000, 200000), jax.random.fold_in(seeds[4], 1), 2000, 199999).astype(jnp.int32),
        "col_marg": with_ends(jax.random.randint(seeds[5], (BANDS, BAND), 2000, 200000), jax.random.fold_in(seeds[5], 1), 2000, 199999).astype(jnp.int32),
        "log_total": jnp.clip(jax.random.uniform(seeds[6], (1,), jnp.float32, 18.0, 22.0), 18.0, 22.0),
    }


def cell_slope(scores, count_part, log_row_part, log_col_all, log_base):
    count_values = count_part.astype(jnp.float32)
    log_ratio = jnp.log(jnp.maximum(count_values, 1.0)) + (log_base - log_row_part[:, None] - log_col_all[None, :])
    score_gap = scores - log_ratio
    return jnp.where(count_part > 0, (0.1 + 0.25 * jnp.sqrt(count_values)) * score_gap, jax.nn.sigmoid(score_gap))

def reference(row_embed, col_embed, counts, occupancy, row_marg, col_marg, log_total):
    col_matrix = col_embed.reshape(D, COLS)
    count_matrix = counts.reshape(ROWS, COLS)
    occ_matrix = occupancy.reshape(ROW_TILES, COLS // TILE).astype(jnp.float32)
    log_col_all = jnp.log(col_marg.reshape(COLS).astype(jnp.float32))
    log_row = jnp.log(row_marg.astype(jnp.float32))
    log_base = log_total[0]
    block_tiles = ROW_DEV // TILE

    def row_block(col_total, block_index):
        first_row = (block_index * ROW_DEV).astype(jnp.int32)
        row_part = lax.dynamic_slice_in_dim(row_embed, first_row, ROW_DEV, 1)
        count_part = lax.dynamic_slice_in_dim(count_matrix, first_row, ROW_DEV, 0)
        log_row_part = lax.dynamic_slice_in_dim(log_row, first_row, ROW_DEV, 0)
        occ_part = lax.dynamic_slice_in_dim(occ_matrix, (block_index * block_tiles).astype(jnp.int32), block_tiles, 0)
        scores = jnp.dot(row_part.T, col_matrix, preferred_element_type=jnp.float32)
        slopes = cell_slope(scores, count_part, log_row_part, log_col_all, log_base)
        masked = slopes.reshape(block_tiles, TILE, COLS // TILE, TILE) * occ_part[:, None, :, None]
        residual = masked.reshape(ROW_DEV, COLS).astype(jnp.bfloat16)
        row_grads = jnp.dot(col_matrix, residual.T, preferred_element_type=jnp.float32)
        col_total = col_total + jnp.dot(row_part, residual, preferred_element_type=jnp.float32)
        return (col_total, row_grads)
    col_total, row_grads = lax.scan(row_block, jnp.zeros((D, COLS), jnp.float32), jnp.arange(ROWS // ROW_DEV, dtype=jnp.int32))
    grad_rows = row_grads.transpose(1, 0, 2).reshape(D, ROWS) * (1.0 / math.sqrt(COLS))
    grad_cols = (col_total * (1.0 / math.sqrt(ROWS))).reshape(D, BANDS, BAND)
    return (grad_rows, grad_cols)
```

```python
import functools
import math

import jax
import jax.numpy as jnp
from jax import lax
from jax.experimental import pallas as pl
from jax.experimental.pallas import tpu as pltpu
from jax.sharding import PartitionSpec as P

LANES = 128
SEND = jnp.bfloat16


def nt(a, b):
    return lax.dot_general(a, b, (((1,), (1,)), ((), ())), preferred_element_type=jnp.float32)


def nn(a, b):
    return lax.dot_general(a, b, (((1,), (0,)), ((), ())), preferred_element_type=jnp.float32)


def split3(x):
    hi = x.astype(jnp.bfloat16).astype(jnp.float32)
    rest = x - hi
    mid = rest.astype(jnp.bfloat16).astype(jnp.float32)
    return hi, mid, rest - mid


def eye(n):
    r = lax.broadcasted_iota(jnp.int32, (n, n), 0)
    c = lax.broadcasted_iota(jnp.int32, (n, n), 1)
    return (r == c).astype(jnp.float32).astype(jnp.bfloat16)


def slope_terms(code):
    slope = jnp.where(code > 0.0, 0.1 + 0.25 * jnp.sqrt(jnp.maximum(code, 0.0)), 0.0)
    return slope, jnp.log(jnp.maximum(code, 1.0))


def cell(code, slope, logc, gap):
    return jnp.where(code == 0.0, jax.nn.sigmoid(gap), slope * (gap - logc))


def repeat(n, fn):
    if n == 1:
        fn(0)
    else:
        pl.loop(0, n)(fn)


def kernel(cfg, r_hbm, c_hbm, cnt_hbm, occ_hbm, rm_hbm, cm_hbm, lt_ref,
           rows_out, cols_out,
           r_v, cnt_v, raug, blk, cg, cd, enc, slope_v, logc_v, res, gcol, s1buf, s2src, s2buf,
           c_ref, occ_ref, rm_ref, cm_ref, dsem, e_s, e_r, gx_s, gx_r, g_s, g_r, w_r, m_s, m_r,
           a_s, a_r, b_s, b_r, token):
    n, d, dp, w, band, rows, tile, q_w, scale_r, scale_c = cfg
    half = n // 2
    hh = half // 2
    nq = rows // q_w
    btiles = band // LANES
    sub = min(band, 256)
    nsub = band // sub
    gcols = band // 2
    subg = min(gcols, 256)
    nsubg = gcols // subg
    me = lax.axis_index("row")
    col = lax.axis_index("col")
    core = lax.rem(me, 2)
    mate = me + 1 - 2 * core
    mine = me // 2
    own_half = mine // hh
    halves = (own_half, 1 - own_half)
    froms = [lax.rem(mine - k + half, half) for k in range(1, half)]
    at_mate = (mate, col)
    at_x = (me, 1 - col)

    def place_of(k, c):
        return ((k // hh) * 2 + c) * hh + lax.rem(k, hh)

    spot = place_of(mine, core)

    def rcopy(src, dst, ss, rs, dev):
        return pltpu.make_async_remote_copy(
            src_ref=src, dst_ref=dst, send_sem=ss, recv_sem=rs,
            device_id=dev, device_id_type=pl.DeviceIdType.MESH)

    def signal(sem, dev):
        pl.semaphore_signal(sem, inc=1, device_id=dev, device_id_type=pl.DeviceIdType.MESH)

    def at_peer(k):
        return (2 * k + core, col)

    near = min(4, half)
    later = ((2, mine == 0), (1, (mine == 0) | (mine == 2)), (3, mine < 3))
    earlier = ((0, mine > 0), (2, (mine == 1) | (mine > 2)), (1, mine > 2), (3, mine > 3))

    def each(pairs, fn):
        for k, cond in pairs:
            pl.when(cond)(functools.partial(fn, k))

    far_later = [(k, mine < k) for k in range(near, half)]
    far_earlier = [(k, mine > k) for k in range(near, half - 1)]
    n_earlier = jnp.where(mine == 1, 2, jnp.where(mine == 2, 1, mine))
    n_far = jnp.where(mine < near, half - near, half - 1 - mine)

    barrier = pltpu.get_barrier_semaphore()
    signal(barrier, at_x)
    signal(barrier, at_mate)
    each(later, lambda k: signal(barrier, at_peer(k)))
    each(far_later, lambda k: signal(barrier, at_peer(k)))

    small = []
    step = q_w * btiles
    loads = [pltpu.make_async_copy(
        cnt_hbm.at[pl.ds(q * step, step), :], cnt_v.at[pl.ds(q * step, step), :], dsem.at[q])
        for q in range(nq)]
    for k, (src, dst) in enumerate(((cm_hbm, cm_ref), (c_hbm, c_ref), (occ_hbm, occ_ref),
                                    (rm_hbm, rm_ref))):
        cp = pltpu.make_async_copy(src, dst, dsem.at[nq + 1 + k])
        cp.start()
        small.append(cp)
    for cp in loads:
        cp.start()
    rload = pltpu.make_async_copy(r_hbm, r_v, dsem.at[nq])
    rload.start()

    def enter():
        pl.semaphore_wait(barrier, 2 + n_earlier)
        slot = jnp.minimum(mine, near)
        each(earlier, lambda k: signal(token.at[slot], at_peer(k)))
        each(far_earlier, lambda k: signal(token.at[slot], at_peer(k)))

    pl.when(mine >= 2)(enter)
    for cp in small:
        cp.wait()

    log_c = jnp.log(cm_ref[...].astype(jnp.float32))
    ri = lax.broadcasted_iota(jnp.int32, (w, w), 0)
    ci = lax.broadcasted_iota(jnp.int32, (w, w), 1)
    log_c = jnp.sum(jnp.where(ri == ci, jnp.broadcast_to(log_c, (w, w)), 0.0), axis=1, keepdims=True)
    hi, mid, lo = split3(log_c)
    blk[...] = jnp.zeros_like(blk)
    blk[:, pl.ds(0, d)] = c_ref[...].astype(jnp.float32)
    li = lax.broadcasted_iota(jnp.int32, (w, dp), 1)
    own = blk[...]
    for at, val in ((d, hi), (d + 1, mid), (d + 2, lo)):
        own = jnp.where(li == at, val, own)
    own = jnp.where((li >= d + 3) & (li < d + 6), 1.0, own)
    cg[0, spot] = own.astype(jnp.bfloat16)

    ident = eye(LANES)

    def encode(q):
        loads[q].wait()
        for t in range(btiles):
            cells = []
            for u in range(q_w // tile):
                x = cnt_v[pl.ds(q * step + u * tile * btiles + t, tile, stride=btiles), :]
                k = q * (q_w // tile) + u
                on = jnp.broadcast_to(occ_ref[t:t + 1, k:k + 1], (tile, LANES)) != 0
                cells.append(jnp.where(on, x, -1).astype(jnp.float32).astype(jnp.bfloat16))
            code = nt(ident, jnp.concatenate(cells, axis=0))
            slope, logc = slope_terms(code)
            for r in range(LANES // w):
                b = t * (LANES // w) + r
                k = b // 2
                at = pl.ds((((k // hh) * 2 + b % 2) * hh + k % hh) * w, w)
                part = slice(r * w, (r + 1) * w)
                enc[0, q, at, :] = code[part].astype(jnp.bfloat16)
                slope_v[q, at, :] = slope[part]
                logc_v[q, at, :] = logc[part]

    ecopies = [rcopy(enc.at[0, q], enc.at[1, q], e_s, e_r.at[q], at_x) for q in range(nq)]
    xcp = rcopy(cg.at[0, spot], cg.at[1, spot], gx_s, gx_r, at_x)

    def to_near(which, waiting):
        def one(k):
            if waiting:
                pl.semaphore_wait(token.at[k], 1)
            if k == 2:
                rcopy(cg.at[which, spot], cg.at[which, spot], g_s, w_r.at[which],
                      at_peer(k)).start()
            else:
                direct(which, k)

        each(later, one)

    def direct(which, k):
        rcopy(cg.at[which, spot], cg.at[which, spot], g_s, g_r.at[which, own_half],
              at_peer(k)).start()

    def to_earlier(which):
        each(earlier, functools.partial(direct, which))
        each(far_earlier, functools.partial(direct, which))

    def to_far(which):
        for k, cond in far_later:
            pl.when(cond & (mine > 0))(functools.partial(direct, which, k))

    def far_ready():
        @pl.when(n_far > 0)
        def _():
            pl.semaphore_wait(token.at[near], n_far)

    def relay(which):
        @pl.when(mine == 2)
        def _():
            at = cg.at[which, place_of(0, core)]
            rcopy(at, at, g_s, w_r.at[which], at_mate).wait_recv()
            for k in range(near, half):
                rcopy(at, at, g_s, g_r.at[which, 0], at_peer(k)).start()

    def begin():
        xcp.start()
        to_earlier(0)

    pl.when(mine >= 2)(begin)
    encode(0)

    @pl.when(mine < 2)
    def _():
        enter()
        begin()

    ecopies[0].start()
    if nq > 1:
        encode(1)
    to_near(0, True)
    if nq > 1:
        ecopies[1].start()
    if nq > 2:
        encode(2)
    pl.when(mine > 0)(far_ready)
    to_far(0)
    relay(0)
    if nq > 2:
        ecopies[2].start()
    for q in range(3, nq):
        encode(q)
        if q > 3:
            ecopies[q - 1].start()
    xcp.wait_recv()
    to_earlier(1)
    to_near(1, False)
    to_far(1)
    if nq > 3:
        ecopies[nq - 1].start()

    rload.wait()
    raug[pl.ds(0, d), :] = r_v[...]
    first = (d // 16) * 16
    row_term = jnp.log(rm_ref[...].astype(jnp.float32)) - lt_ref[0]
    hi, mid, lo = split3(row_term)
    tail = raug[pl.ds(first, dp - first), :].astype(jnp.float32)
    si = lax.broadcasted_iota(jnp.int32, (dp - first, rows), 0) + first
    tail = jnp.where(si < d, tail, jnp.where(si < d + 3, 1.0, 0.0))
    for at, val in ((d + 3, hi), (d + 4, mid), (d + 5, lo)):
        tail = jnp.where(si == at, val, tail)
    raug[pl.ds(first, dp - first), :] = tail.astype(jnp.bfloat16)

    def arrived(which, h, blocks):
        some = cg.at[which, pl.ds(0, blocks)]
        rcopy(some, some, g_s, g_r.at[which, h], at_mate).wait_recv()

    def to_mate(which, h):
        part = cg.at[which, pl.ds((h * 2 + core) * hh, hh)]
        return rcopy(part, part, m_s, m_r.at[which, h], at_mate)

    def gathered(which, at):
        h = halves[at]
        if at:
            arrived(which, h, hh)
        else:
            pl.when(mine == 2)(lambda: arrived(which, h, hh - 2))
            pl.when(mine != 2)(lambda: arrived(which, h, hh - 1))
        to_mate(which, h).start()

    def block(which, first, count):
        return cg[which, pl.ds(first, count)].reshape(count * w, dp)

    def reduced(k):
        return rcopy(s2src.at[k], s2buf.at[mine], b_s, b_r, at_peer(k))

    def from_mate(h):
        return rcopy(gcol.at[pl.ds((h * 2 + 1 - core) * hh, hh)], s1buf.at[pl.ds(h * hh, hh)],
                     a_s, a_r.at[h], at_mate)

    def half_terms(h):
        for q in range(nq):
            qs = pl.ds(q * q_w, q_w)

            def cells(s):
                at = pl.ds(pl.multiple_of(h * gcols + s * subg, subg), subg)
                gap = nn(block(0, (h * gcols + s * subg) // w, subg // w), raug[:, qs])
                code = enc[0, q, at, :].astype(jnp.float32)
                res[at, qs] = cell(code, slope_v[q, at, :], logc_v[q, at, :], gap).astype(jnp.bfloat16)

            repeat(nsubg, cells)

        def terms(s):
            at = pl.ds(pl.multiple_of(h * gcols + s * subg, subg), subg)
            part = nt(res[at, :], raug[...]).reshape(subg // w, w, dp)
            gcol[pl.ds((h * gcols + s * subg) // w, subg // w)] = part

        repeat(nsubg, terms)

    def spread(h, own):
        from_mate(h).wait_recv()
        for i in range(hh):
            k = h * hh + i
            total = gcol[(h * 2 + core) * hh + i] + s1buf[k]
            s2src[k] = total.astype(s2src.dtype)
            if own:
                @pl.when(mine == k)
                def _():
                    blk[...] = total

            if i and own:
                pl.when(mine != k - 1)(lambda: reduced(k - 1).start())
            elif i:
                reduced(k - 1).start()

    def spread_last(h, own):
        k = h * hh + hh - 1
        if own:
            pl.when(mine != k)(lambda: reduced(k).start())
        else:
            reduced(k).start()

    ident_d = eye(dp)

    def transposed(which):
        def one(s):
            part = block(which, s * (sub // w), sub // w)
            cd[which, :, pl.ds(s * sub, sub)] = nt(ident_d, part).astype(jnp.bfloat16)

        repeat(nsub, one)

    gathered(0, 0)
    to_mate(0, own_half).wait_recv()
    half_terms(own_half)
    from_mate(own_half).start()
    gathered(0, 1)
    relay(1)
    to_mate(0, 1 - own_half).wait_recv()
    half_terms(1 - own_half)
    pl.when(mine == 0)(far_ready)
    from_mate(1 - own_half).start()
    spread(own_half, True)
    gathered(1, 0)
    spread_last(own_half, True)
    transposed(0)
    spread(1 - own_half, False)
    gathered(1, 1)
    spread_last(1 - own_half, False)
    rows_out[...] = nn(cd[0], res[...])[:d, :]

    to_mate(1, own_half).wait_recv()
    to_mate(1, 1 - own_half).wait_recv()
    transposed(1)
    for q in range(nq):
        qs = pl.ds(q * q_w, q_w)
        ecopies[q].wait_recv()

        def cells(s):
            at = pl.ds(s * sub, sub)
            gap = nn(block(1, s * (sub // w), sub // w), raug[:, qs])
            code = enc[1, q, at, :].astype(jnp.float32)
            slope, logc = slope_terms(code)
            res[at, qs] = cell(code, slope, logc, gap).astype(jnp.bfloat16)

        repeat(nsub, cells)
        rows_out[:, qs] = (rows_out[:, qs] + nn(cd[1], res[:, qs])[:d, :]) * scale_r

    got = s2buf.at[pl.ds(0, half - 1)]
    summed = rcopy(got, got, b_s, b_r, at_mate)
    summed.wait_recv()
    total = blk[...]
    for k in froms:
        total = total + s2buf[k].astype(jnp.float32)
    cols_out[...] = (total * scale_c)[:, :d]

    def sent(blocks):
        some = gcol.at[pl.ds(0, blocks)]
        rcopy(some, some, g_s, gx_r, at_mate).wait_send()

    pl.when(mine == 0)(lambda: sent(near - 1))
    pl.when(mine == 2)(lambda: sent(2 * half - 1 - near))
    pl.when((mine != 0) & (mine != 2))(lambda: sent(half - 1))
    xcp.wait_send()
    rcopy(cg.at[0], cg.at[1], m_s, gx_r, at_mate).wait_send()
    rcopy(enc.at[0], enc.at[1], e_s, gx_r, at_x).wait_send()
    some = gcol.at[pl.ds(0, half)]
    rcopy(some, some, a_s, gx_r, at_mate).wait_send()
    summed.wait_send()


def scratch_bytes(shapes):
    return sum(math.prod(s.shape) * jnp.dtype(s.dtype).itemsize for s in shapes)


def place(rows_in, cols_in, rows_out, cols_out, sem):
    copies = [pltpu.make_async_copy(rows_in, rows_out, sem.at[0]),
              pltpu.make_async_copy(cols_in, cols_out, sem.at[1])]
    for cp in copies:
        cp.start()
    for cp in copies:
        cp.wait()


def body(row_embed, col_embed, counts, occupancy, row_marg, col_marg, log_total):
    n = lax.axis_size("row")
    d, rows = row_embed.shape
    w = col_embed.shape[2]
    band = counts.shape[2]
    tile = rows // occupancy.shape[0]
    q_w = 2 * tile if rows % (2 * tile) == 0 else tile
    dp = -(-(d + 6) // LANES) * LANES
    half = n // 2
    nq = rows // q_w
    btiles = band // LANES
    cfg = (n, d, dp, w, band, rows, tile, q_w,
           1.0 / math.sqrt(w * n * lax.axis_size("col")), 1.0 / math.sqrt(rows * n))
    bf, f32 = jnp.bfloat16, jnp.float32
    vm, hb, anywhere = (pl.BlockSpec(memory_space=m) for m in (pltpu.VMEM, pltpu.HBM, pl.ANY))
    dma = lambda *s: pltpu.SemaphoreType.DMA(s) if s else pltpu.SemaphoreType.DMA
    scratch = [
        pltpu.VMEM((d, rows), bf),
        pltpu.VMEM((rows * btiles, LANES), jnp.int32),
        pltpu.VMEM((dp, rows), bf),
        pltpu.VMEM((w, dp), f32),
        pltpu.VMEM((2, n, w, dp), bf),
        pltpu.VMEM((2, dp, band), bf),
        pltpu.VMEM((2, nq, band, q_w), bf),
        pltpu.VMEM((nq, band, q_w), f32),
        pltpu.VMEM((nq, band, q_w), f32),
        pltpu.VMEM((band, rows), bf),
        pltpu.VMEM((n, w, dp), f32),
        pltpu.VMEM((half, w, dp), f32),
        pltpu.VMEM((half, w, dp), SEND),
        pltpu.VMEM((half, w, dp), SEND),
        pltpu.VMEM((w, d), bf),
        pltpu.VMEM((occupancy.shape[2], occupancy.shape[0]), jnp.int32),
        pltpu.VMEM((1, rows), jnp.int32),
        pltpu.VMEM((1, w), jnp.int32),
        dma(nq + 5),
        dma(), dma(nq), dma(), dma(), dma(), dma(2, 2), dma(2), dma(), dma(2, 2),
        dma(), dma(2), dma(), dma(),
        pltpu.SemaphoreType.REGULAR((5,)),
    ]
    limit = min(60 << 20, (6 << 20) + scratch_bytes(scratch[:18]) + 2 * d * rows * 4 + 24 * band * q_w)
    grad_rows, grad_cols = pl.pallas_call(
        functools.partial(kernel, cfg),
        out_shape=(jax.ShapeDtypeStruct((d, rows), f32), jax.ShapeDtypeStruct((w, d), f32)),
        in_specs=[hb] * 6 + [pl.BlockSpec(memory_space=pltpu.SMEM)],
        out_specs=(vm, vm),
        scratch_shapes=scratch,
        compiler_params=pltpu.CompilerParams(
            collective_id=0, has_side_effects=True, vmem_limit_bytes=limit),
    )(
        *(pltpu.with_memory_space_constraint(x, pltpu.HBM) for x in (
            row_embed,
            jnp.transpose(col_embed, (1, 2, 0)).reshape(w, d),
            counts.reshape(rows * btiles, LANES),
            jnp.transpose(occupancy, (1, 2, 0)).reshape(occupancy.shape[2], occupancy.shape[0]),
            row_marg.reshape(1, rows),
            col_marg,
        )),
        log_total,
    )
    grad_rows, grad_cols = pl.pallas_call(
        place,
        out_shape=(jax.ShapeDtypeStruct((d, rows), f32), jax.ShapeDtypeStruct((w, d), f32)),
        in_specs=[anywhere, anywhere],
        out_specs=(hb, hb),
        scratch_shapes=[pltpu.SemaphoreType.DMA((2,))],
    )(*(pltpu.with_memory_space_constraint(x, pltpu.VMEM) for x in (grad_rows, grad_cols)))
    return grad_rows, jnp.transpose(grad_cols.reshape(1, w, d), (2, 0, 1))


def solution(mesh):
    placed = (
        P(None, "row"),
        P(None, "col", "row"),
        P("row", "col", None),
        P("row", "col", None),
        P("row"),
        P("col", "row"),
        P(),
    )
    return jax.shard_map(
        body,
        mesh=mesh,
        in_specs=placed,
        out_specs=(P(None, "row"), P(None, "col", "row")),
        check_vma=False,
    )
```

```python
import functools
import math

import jax
import jax.numpy as jnp
from jax import lax
from jax.experimental import pallas as pl
from jax.experimental.pallas import tpu as pltpu
from jax.sharding import PartitionSpec as P

LANES = 128
SEND = jnp.bfloat16


def nt(a, b):
    return lax.dot_general(a, b, (((1,), (1,)), ((), ())), preferred_element_type=jnp.float32)


def nn(a, b):
    return lax.dot_general(a, b, (((1,), (0,)), ((), ())), preferred_element_type=jnp.float32)


def split3(x):
    hi = x.astype(jnp.bfloat16).astype(jnp.float32)
    rest = x - hi
    mid = rest.astype(jnp.bfloat16).astype(jnp.float32)
    return hi, mid, rest - mid


def eye(n):
    r = lax.broadcasted_iota(jnp.int32, (n, n), 0)
    c = lax.broadcasted_iota(jnp.int32, (n, n), 1)
    return (r == c).astype(jnp.float32).astype(jnp.bfloat16)


def slope_terms(code):
    slope = jnp.where(code > 0.0, 0.1 + 0.25 * jnp.sqrt(jnp.maximum(code, 0.0)), 0.0)
    return slope, jnp.log(jnp.maximum(code, 1.0))


def cell(code, slope, logc, gap):
    return jnp.where(code == 0.0, jax.nn.sigmoid(gap), slope * (gap - logc))


def repeat(n, fn):
    if n == 1:
        fn(0)
    else:
        pl.loop(0, n)(fn)


def kernel(cfg, r_hbm, c_hbm, cnt_hbm, occ_hbm, rm_hbm, cm_hbm, lt_ref,
           rows_out, cols_out,
           r_v, cnt_v, raug, blk, cg, cd, enc, slope_v, logc_v, res, gcol, s1buf, s2src, s2buf,
           c_ref, occ_ref, rm_ref, cm_ref, dsem, e_s, e_r, gx_s, gx_r, g_s, g_r, w_s, w_r, m_s, m_r,
           a_s, a_r, b_s, b_r, token, x_token, c_s, c_r, s0src, s0buf, res0):
    n, d, dp, w, band, rows, tile, q_w, scale_r, scale_c = cfg
    half = n // 2
    dq = -(-d // 16) * 16
    hh = half // 2
    nq = rows // q_w
    btiles = band // LANES
    sub = min(band, 256)
    nsub = band // sub
    gcols = band // 2
    subg = min(gcols, 256)
    nsubg = gcols // subg
    me = lax.axis_index("row")
    col = lax.axis_index("col")
    core = lax.rem(me, 2)
    mate = me + 1 - 2 * core
    mine = me // 2
    own_half = mine // hh
    halves = (own_half, 1 - own_half)
    froms = [lax.rem(mine - k + half, half) for k in range(1, half)]
    at_mate = (mate, col)
    at_x = (me, 1 - col)

    def place_of(k, c):
        return ((k // hh) * 2 + c) * hh + lax.rem(k, hh)

    spot = place_of(mine, core)

    def rcopy(src, dst, ss, rs, dev):
        return pltpu.make_async_remote_copy(
            src_ref=src, dst_ref=dst, send_sem=ss, recv_sem=rs,
            device_id=dev, device_id_type=pl.DeviceIdType.MESH)

    def signal(sem, dev):
        pl.semaphore_signal(sem, inc=1, device_id=dev, device_id_type=pl.DeviceIdType.MESH)

    def at_peer(k):
        return (2 * k + core, col)

    near = hh
    later = [(2, mine == 0), (1, (mine == 0) | (mine == 2))]
    later += [(k, mine < k) for k in range(3, near)]
    earlier = [(0, mine > 0), (2, (mine == 1) | (mine > 2)), (1, mine > 2)]
    earlier += [(k, mine > k) for k in range(3, near)]

    def each(pairs, fn):
        for k, cond in pairs:
            pl.when(cond)(functools.partial(fn, k))

    far_later = [(k, mine < k) for k in range(near, half)]
    far_earlier = [(k, mine > k) for k in range(near, half - 1)]
    n_earlier = jnp.where(mine == 1, 2, jnp.where(mine == 2, 1, mine))
    n_far = jnp.where(mine < near, half - near, half - 1 - mine)

    barrier = pltpu.get_barrier_semaphore()
    pl.when(col == 0)(lambda: signal(barrier, at_x))
    signal(barrier, at_mate)
    each(later, lambda k: signal(barrier, at_peer(k)))
    each(far_later, lambda k: signal(barrier, at_peer(k)))

    small = []
    step = q_w * btiles
    loads = [pltpu.make_async_copy(
        cnt_hbm.at[pl.ds(q * step, step), :], cnt_v.at[pl.ds(q * step, step), :], dsem.at[q])
        for q in range(nq)]
    for k, (src, dst) in enumerate(((cm_hbm, cm_ref), (c_hbm, c_ref), (occ_hbm, occ_ref),
                                    (rm_hbm, rm_ref))):
        cp = pltpu.make_async_copy(src, dst, dsem.at[nq + 1 + k])
        cp.start()
        small.append(cp)
    for cp in loads:
        cp.start()
    rload = pltpu.make_async_copy(r_hbm, r_v, dsem.at[nq])

    pl.semaphore_wait(barrier, 1 + col + n_earlier)
    slot = jnp.minimum(mine, near)
    pl.when(col == 1)(lambda: signal(x_token, at_x))
    each(earlier, lambda k: signal(token.at[slot], at_peer(k)))
    each(far_earlier, lambda k: signal(token.at[slot], at_peer(k)))

    for cp in small:
        cp.wait()

    log_c = jnp.log(cm_ref[...].astype(jnp.float32))
    ri = lax.broadcasted_iota(jnp.int32, (w, w), 0)
    ci = lax.broadcasted_iota(jnp.int32, (w, w), 1)
    log_c = jnp.sum(jnp.where(ri == ci, jnp.broadcast_to(log_c, (w, w)), 0.0), axis=1, keepdims=True)
    hi, mid, lo = split3(log_c)
    blk[...] = jnp.zeros_like(blk)
    blk[:, pl.ds(0, d)] = c_ref[...].astype(jnp.float32)
    li = lax.broadcasted_iota(jnp.int32, (w, dp), 1)
    own = blk[...]
    for at, val in ((d, hi), (d + 1, mid), (d + 2, lo)):
        own = jnp.where(li == at, val, own)
    own = jnp.where((li >= d + 3) & (li < d + 6), 1.0, own)
    cg[0, spot] = own.astype(jnp.bfloat16)

    ident = eye(LANES)

    def encode(q):
        loads[q].wait()
        for t in range(btiles):
            cells = []
            for u in range(q_w // tile):
                x = cnt_v[pl.ds(q * step + u * tile * btiles + t, tile, stride=btiles), :]
                k = q * (q_w // tile) + u
                on = jnp.broadcast_to(occ_ref[t:t + 1, k:k + 1], (tile, LANES)) != 0
                cells.append(jnp.where(on, x, -1).astype(jnp.float32).astype(jnp.bfloat16))
            code = nt(ident, jnp.concatenate(cells, axis=0))
            slope, logc = slope_terms(code)
            for r in range(LANES // w):
                b = t * (LANES // w) + r
                k = b // 2
                at = pl.ds((((k // hh) * 2 + b % 2) * hh + k % hh) * w, w)
                some = slice(r * w, (r + 1) * w)
                enc[0, q, at, :] = code[some].astype(jnp.bfloat16)
                slope_v[q, at, :] = slope[some]
                logc_v[q, at, :] = logc[some]

    def x_start(q, part):
        at = pl.ds(pl.multiple_of(part * gcols, gcols), gcols)
        rcopy(enc.at[0, q, at], enc.at[1, q, at], e_s, e_r.at[q], at_x).start()

    ecopies = [rcopy(enc.at[0, q], enc.at[1, q], e_s, e_r.at[q], at_x) for q in range(nq)]
    xcp = rcopy(cg.at[0, spot], cg.at[1, spot], gx_s, gx_r, at_x)

    def to_near(which, waiting):
        def one(k):
            if waiting:
                pl.semaphore_wait(token.at[k], 1)
            if k == 2:
                rcopy(cg.at[which, spot], cg.at[which, spot], g_s, w_r.at[which],
                      at_peer(k)).start()
            else:
                direct(which, k)

        each(later, one)

    def direct(which, k):
        rcopy(cg.at[which, spot], cg.at[which, spot], g_s, g_r.at[which, own_half],
              at_peer(k)).start()

    def to_earlier(which):
        each(earlier, functools.partial(direct, which))
        each(far_earlier, functools.partial(direct, which))

    def to_far(which):
        for k, cond in far_later:
            pl.when(cond & (mine > 0))(functools.partial(direct, which, k))

    def far_ready():
        @pl.when(n_far > 0)
        def _():
            pl.semaphore_wait(token.at[near], n_far)

    def relay(which):
        @pl.when(mine == 2)
        def _():
            at = cg.at[which, place_of(0, core)]
            rcopy(at, at, w_s, w_r.at[which], at_mate).wait_recv()
            for k in range(near, half):
                if which:
                    rcopy(at, at, w_s, g_r.at[which, 0], at_peer(k)).start()
                else:
                    for c in range(2):
                        rcopy(at, at, w_s, w_r.at[which], (2 * k + c, col)).start()

    to_earlier(0)
    encode(0)

    @pl.when(mine >= near)
    def _():
        far_ready()
        to_far(0)

    pl.when(col == 0)(lambda: pl.semaphore_wait(x_token, 1))
    xcp.start()
    x_start(0, 0)
    x_start(0, 1)
    if nq > 2:
        encode(1)
    to_near(0, True)

    @pl.when((mine > 0) & (mine < near))
    def _():
        far_ready()
        to_far(0)

    relay(0)
    rload.start()
    for q in range(2, nq):
        x_start(q - 1, 0)
        x_start(q - 1, 1)
        encode(q)
    xcp.wait_recv()
    to_earlier(1)
    to_near(1, False)
    to_far(1)

    rload.wait()
    raug[pl.ds(0, d), :] = r_v[...]
    first = (d // 16) * 16
    row_term = jnp.log(rm_ref[...].astype(jnp.float32)) - lt_ref[0]
    hi, mid, lo = split3(row_term)
    tail = raug[pl.ds(first, dp - first), :].astype(jnp.float32)
    si = lax.broadcasted_iota(jnp.int32, (dp - first, rows), 0) + first
    tail = jnp.where(si < d, tail, jnp.where(si < d + 3, 1.0, 0.0))
    for at, val in ((d + 3, hi), (d + 4, mid), (d + 5, lo)):
        tail = jnp.where(si == at, val, tail)
    raug[pl.ds(first, dp - first), :] = tail.astype(jnp.bfloat16)

    def arrived(which, h, blocks):
        some = cg.at[which, pl.ds(0, blocks)]
        rcopy(some, some, g_s, g_r.at[which, h], at_mate).wait_recv()

    def to_mate(which, h, skip):
        part = cg.at[which, pl.ds((h * 2 + core) * hh + skip, hh - skip)]
        return rcopy(part, part, m_s, m_r.at[which, h], at_mate)

    def gathered(which, at):
        h = halves[at]

        def took(blocks, skip):
            arrived(which, h, blocks)
            to_mate(which, h, skip).start()

        if at and which:
            took(hh, 0)
        elif at:
            pl.when(mine < hh)(lambda: took(hh, 0))
            pl.when(mine >= hh)(lambda: took(hh - 1, 1))
        else:
            pl.when(mine == 2)(lambda: took(hh - 2, 0))
            pl.when(mine != 2)(lambda: took(hh - 1, 0))

    def from_mate_blocks(which, at):
        h = halves[at]
        if at and not which:
            pl.when(mine < hh)(lambda: to_mate(which, h, 0).wait_recv())
            pl.when(mine >= hh)(lambda: to_mate(which, h, 1).wait_recv())
        else:
            to_mate(which, h, 0).wait_recv()

    def first_chip():
        two = cg.at[0, pl.ds(0, 2)]
        rcopy(two, two, w_s, w_r.at[0], at_mate).wait_recv()
        ends = (pl.ds(0, w), pl.ds(hh * w, w))

        def both(fn):
            return jnp.concatenate([fn(at) for at in ends], axis=0)

        blocks = jnp.concatenate([cg[0, 0], cg[0, hh]], axis=0)
        for q in range(nq):
            qs = pl.ds(q * q_w, q_w)
            gap = nn(blocks, raug[:, qs])
            code = both(lambda at: enc[0, q, at, :]).astype(jnp.float32)
            slope = both(lambda at: slope_v[q, at, :])
            logc = both(lambda at: logc_v[q, at, :])
            res0[:, qs] = cell(code, slope, logc, gap).astype(jnp.bfloat16)
        s0src[...] = nt(res0[...], raug[...]).reshape(2, w, dp).astype(jnp.bfloat16)
        spare = (mine - hh) * 2 + core
        for c in range(2):
            rcopy(s0src.at[c], s0buf.at[spare], c_s, c_r, (c, col)).start()

    def block(which, first, count):
        return cg[which, pl.ds(first, count)].reshape(count * w, dp)

    def reduced(k):
        return rcopy(s2src.at[k], s2buf.at[mine], b_s, b_r, at_peer(k))

    def from_mate(h):
        return rcopy(gcol.at[pl.ds((h * 2 + 1 - core) * hh, hh)], s1buf.at[pl.ds(h * hh, hh)],
                     a_s, a_r.at[h], at_mate)

    def half_terms(h):
        for q in range(nq):
            qs = pl.ds(q * q_w, q_w)

            def cells(s):
                at = pl.ds(pl.multiple_of(h * gcols + s * subg, subg), subg)
                gap = nn(block(0, (h * gcols + s * subg) // w, subg // w), raug[:, qs])
                code = enc[0, q, at, :].astype(jnp.float32)
                got = cell(code, slope_v[q, at, :], logc_v[q, at, :], gap).astype(jnp.bfloat16)
                res[at, qs] = got
                if q == nq - 1:
                    enc[0, q, at, :] = got

            repeat(nsubg, cells)

        def terms(s):
            at = pl.ds(pl.multiple_of(h * gcols + s * subg, subg), subg)
            part = nt(res[at, :], raug[...]).reshape(subg // w, w, dp)
            gcol[pl.ds((h * gcols + s * subg) // w, subg // w)] = part

        repeat(nsubg, terms)

    def spread(h, own):
        from_mate(h).wait_recv()
        for i in range(hh):
            k = h * hh + i
            total = gcol[(h * 2 + core) * hh + i] + s1buf[k]
            s2src[k] = total.astype(s2src.dtype)
            if own:
                @pl.when(mine == k)
                def _():
                    blk[...] = total

            if i and own:
                pl.when(mine != k - 1)(lambda: reduced(k - 1).start())
            elif i == 1:
                pl.when(mine < hh)(lambda: reduced(k - 1).start())
            elif i:
                reduced(k - 1).start()

    def spread_last(h, own):
        k = h * hh + hh - 1
        if own:
            pl.when(mine != k)(lambda: reduced(k).start())
        else:
            reduced(k).start()

    ident_d = eye(dp)

    def transposed(which, h):
        def one(s):
            part = block(which, (h * gcols + s * subg) // w, subg // w)
            at = pl.ds(pl.multiple_of(h * gcols + s * subg, subg), subg)
            cd[which, :, at] = nt(ident_d, part).astype(jnp.bfloat16)

        repeat(nsubg, one)

    def other_cells(q, h):
        qs = pl.ds(q * q_w, q_w)

        def cells(s):
            at = pl.ds(pl.multiple_of(h * gcols + s * subg, subg), subg)
            gap = nn(block(1, (h * gcols + s * subg) // w, subg // w), raug[:, qs])
            code = enc[1, q, at, :].astype(jnp.float32)
            slope, logc = slope_terms(code)
            enc[1, q, at, :] = cell(code, slope, logc, gap).astype(jnp.bfloat16)

        repeat(nsubg, cells)

    def other_rows(q):
        qs = pl.ds(q * q_w, q_w)
        more = nn(cd[1, :dq, :], enc[1, q])[:d, :]
        rows_out[:, qs] = (rows_out[:, qs] + more) * scale_r

    gathered(0, 0)
    from_mate_blocks(0, 0)
    half_terms(own_half)
    from_mate(own_half).start()
    x_start(nq - 1, own_half)
    pl.when(mine >= hh)(first_chip)
    gathered(0, 1)
    relay(1)
    from_mate_blocks(0, 1)
    half_terms(1 - own_half)
    pl.when(mine == 0)(far_ready)
    from_mate(1 - own_half).start()
    x_start(nq - 1, 1 - own_half)
    spread(own_half, True)
    gathered(1, 0)
    spread_last(own_half, True)
    transposed(0, 0)
    transposed(0, 1)
    spread(1 - own_half, False)
    spread_last(1 - own_half, False)
    rows_out[...] = nn(cd[0, :dq, :], res[...])[:d, :]

    from_mate_blocks(1, 0)
    transposed(1, own_half)
    sooner = nq // 2
    for q in range(sooner):
        ecopies[q].wait_recv()
        other_cells(q, own_half)
    gathered(1, 1)
    from_mate_blocks(1, 1)
    transposed(1, 1 - own_half)
    for q in range(sooner):
        other_cells(q, 1 - own_half)
        other_rows(q)
    for q in range(sooner, nq):
        ecopies[q].wait_recv()
        if q < nq - 1:
            other_cells(q, 0)
            other_cells(q, 1)
        other_rows(q)

    def summed(blocks):
        got = s2buf.at[pl.ds(0, blocks)]
        return rcopy(got, got, b_s, b_r, at_mate)

    @pl.when(mine == 0)
    def _():
        summed(hh - 1).wait_recv()
        total = blk[...]
        for k in range(1, hh):
            total = total + s2buf[k].astype(jnp.float32)
        rcopy(s0buf, s0buf, c_s, c_r, at_mate).wait_recv()
        for k in range(half):
            total = total + s0buf[k].astype(jnp.float32)
        cols_out[...] = (total * scale_c)[:, :d]

    @pl.when(mine != 0)
    def _():
        summed(half - 1).wait_recv()
        total = blk[...]
        for k in froms:
            total = total + s2buf[k].astype(jnp.float32)
        cols_out[...] = (total * scale_c)[:, :d]

    def sent(blocks):
        some = gcol.at[pl.ds(0, blocks)]
        rcopy(some, some, g_s, gx_r, at_mate).wait_send()

    pl.when(mine == 0)(lambda: sent(near - 1))
    pl.when(mine != 0)(lambda: sent(half - 1))

    @pl.when(mine == 2)
    def _():
        some = gcol.at[pl.ds(0, 3 * (half - near) // 2)]
        rcopy(some, some, w_s, gx_r, at_mate).wait_send()

    xcp.wait_send()
    def told(blocks):
        some = cg.at[0, pl.ds(0, blocks)]
        rcopy(some, some, m_s, gx_r, at_mate).wait_send()

    pl.when(mine < hh)(lambda: told(n))
    pl.when(mine >= hh)(lambda: told(n - 1))
    rcopy(enc.at[0], enc.at[1], e_s, gx_r, at_x).wait_send()
    some = gcol.at[pl.ds(0, half)]
    rcopy(some, some, a_s, gx_r, at_mate).wait_send()
    pl.when(mine < hh)(lambda: summed(half - 1).wait_send())

    @pl.when(mine >= hh)
    def _():
        summed(half - 2).wait_send()
        rcopy(s0src, s0src, c_s, c_r, at_mate).wait_send()


def scratch_bytes(shapes):
    return sum(math.prod(s.shape) * jnp.dtype(s.dtype).itemsize for s in shapes)


def place(rows_in, cols_in, rows_out, cols_out, sem):
    copies = [pltpu.make_async_copy(rows_in, rows_out, sem.at[0]),
              pltpu.make_async_copy(cols_in, cols_out, sem.at[1])]
    for cp in copies:
        cp.start()
    for cp in copies:
        cp.wait()


def body(row_embed, col_embed, counts, occupancy, row_marg, col_marg, log_total):
    n = lax.axis_size("row")
    d, rows = row_embed.shape
    w = col_embed.shape[2]
    band = counts.shape[2]
    tile = rows // occupancy.shape[0]
    q_w = 2 * tile if rows % (2 * tile) == 0 else tile
    dp = -(-(d + 6) // LANES) * LANES
    half = n // 2
    nq = rows // q_w
    btiles = band // LANES
    cfg = (n, d, dp, w, band, rows, tile, q_w,
           1.0 / math.sqrt(w * n * lax.axis_size("col")), 1.0 / math.sqrt(rows * n))
    bf, f32 = jnp.bfloat16, jnp.float32
    vm, hb, anywhere = (pl.BlockSpec(memory_space=m) for m in (pltpu.VMEM, pltpu.HBM, pl.ANY))
    dma = lambda *s: pltpu.SemaphoreType.DMA(s) if s else pltpu.SemaphoreType.DMA
    scratch = [
        pltpu.VMEM((d, rows), bf),
        pltpu.VMEM((rows * btiles, LANES), jnp.int32),
        pltpu.VMEM((dp, rows), bf),
        pltpu.VMEM((w, dp), f32),
        pltpu.VMEM((2, n, w, dp), bf),
        pltpu.VMEM((2, dp, band), bf),
        pltpu.VMEM((2, nq, band, q_w), bf),
        pltpu.VMEM((nq, band, q_w), f32),
        pltpu.VMEM((nq, band, q_w), f32),
        pltpu.VMEM((band, rows), bf),
        pltpu.VMEM((n, w, dp), f32),
        pltpu.VMEM((half, w, dp), f32),
        pltpu.VMEM((half, w, dp), SEND),
        pltpu.VMEM((half, w, dp), SEND),
        pltpu.VMEM((w, d), bf),
        pltpu.VMEM((occupancy.shape[2], occupancy.shape[0]), jnp.int32),
        pltpu.VMEM((1, rows), jnp.int32),
        pltpu.VMEM((1, w), jnp.int32),
        dma(nq + 5),
        dma(), dma(nq), dma(), dma(), dma(), dma(2, 2), dma(), dma(2), dma(), dma(2, 2),
        dma(), dma(2), dma(), dma(),
        pltpu.SemaphoreType.REGULAR((half // 2 + 1,)),
        pltpu.SemaphoreType.REGULAR,
        dma(), dma(),
        pltpu.VMEM((2, w, dp), bf),
        pltpu.VMEM((half, w, dp), bf),
        pltpu.VMEM((2 * w, rows), bf),
    ]
    limit = min(60 << 20, (6 << 20) + scratch_bytes(scratch[:18]) + 2 * d * rows * 4 + 28 * band * q_w)
    grad_rows, grad_cols = pl.pallas_call(
        functools.partial(kernel, cfg),
        out_shape=(jax.ShapeDtypeStruct((d, rows), f32), jax.ShapeDtypeStruct((w, d), f32)),
        in_specs=[hb] * 6 + [pl.BlockSpec(memory_space=pltpu.SMEM)],
        out_specs=(vm, vm),
        scratch_shapes=scratch,
        compiler_params=pltpu.CompilerParams(
            collective_id=0, has_side_effects=True, vmem_limit_bytes=limit),
    )(
        *(pltpu.with_memory_space_constraint(x, pltpu.HBM) for x in (
            row_embed,
            jnp.transpose(col_embed, (1, 2, 0)).reshape(w, d),
            counts.reshape(rows * btiles, LANES),
            jnp.transpose(occupancy, (1, 2, 0)).reshape(occupancy.shape[2], occupancy.shape[0]),
            row_marg.reshape(1, rows),
            col_marg,
        )),
        log_total,
    )
    grad_rows, grad_cols = pl.pallas_call(
        place,
        out_shape=(jax.ShapeDtypeStruct((d, rows), f32), jax.ShapeDtypeStruct((w, d), f32)),
        in_specs=[anywhere, anywhere],
        out_specs=(hb, hb),
        scratch_shapes=[pltpu.SemaphoreType.DMA((2,))],
    )(*(pltpu.with_memory_space_constraint(x, pltpu.VMEM) for x in (grad_rows, grad_cols)))
    return grad_rows, jnp.transpose(grad_cols.reshape(1, w, d), (2, 0, 1))


def solution(mesh):
    placed = (
        P(None, "row"),
        P(None, "col", "row"),
        P("row", "col", None),
        P("row", "col", None),
        P("row"),
        P("col", "row"),
        P(),
    )
    return jax.shard_map(
        body,
        mesh=mesh,
        in_specs=placed,
        out_specs=(P(None, "row"), P(None, "col", "row")),
        check_vma=False,
    )
```

```python
import functools
import math

import jax
import jax.numpy as jnp
from jax import lax
from jax.experimental import pallas as pl
from jax.experimental.pallas import tpu as pltpu
from jax.sharding import PartitionSpec as P

LANES = 128
SEND = jnp.bfloat16


def nt(a, b):
    return lax.dot_general(a, b, (((1,), (1,)), ((), ())), preferred_element_type=jnp.float32)


def nn(a, b):
    return lax.dot_general(a, b, (((1,), (0,)), ((), ())), preferred_element_type=jnp.float32)


def split3(x):
    hi = x.astype(jnp.bfloat16).astype(jnp.float32)
    rest = x - hi
    mid = rest.astype(jnp.bfloat16).astype(jnp.float32)
    return hi, mid, rest - mid


def eye(n):
    r = lax.broadcasted_iota(jnp.int32, (n, n), 0)
    c = lax.broadcasted_iota(jnp.int32, (n, n), 1)
    return (r == c).astype(jnp.float32).astype(jnp.bfloat16)


def slope_terms(code):
    slope = jnp.where(code > 0.0, 0.1 + 0.25 * jnp.sqrt(jnp.maximum(code, 0.0)), 0.0)
    return slope, jnp.log(jnp.maximum(code, 1.0))


def cell(code, slope, logc, gap):
    return jnp.where(code == 0.0, jax.nn.sigmoid(gap), slope * (gap - logc))


def repeat(n, fn):
    if n == 1:
        fn(0)
    else:
        pl.loop(0, n)(fn)


def kernel(cfg, r_hbm, c_hbm, cnt_hbm, occ_hbm, rm_hbm, cm_hbm, lt_ref,
           rows_out, cols_out,
           r_v, cnt_v, raug, blk, cg, cd, enc, slope_v, logc_v, res, gcol, s1buf, s2src, s2buf,
           c_ref, occ_ref, rm_ref, cm_ref, dsem, e_s, e_r, gx_s, gx_r, g_s, g_r, w_s, w_r, m_s, m_r,
           a_s, a_r, b_s, b_r, token, x_token, c_s, c_r, s0src, s0buf, res0):
    n, d, dp, w, band, rows, tile, q_w, scale_r, scale_c = cfg
    half = n // 2
    dq = -(-d // 16) * 16
    hh = half // 2
    nq = rows // q_w
    btiles = band // LANES
    sub = min(band, 256)
    nsub = band // sub
    gcols = band // 2
    subg = min(gcols, 256)
    nsubg = gcols // subg
    me = lax.axis_index("row")
    col = lax.axis_index("col")
    core = lax.rem(me, 2)
    mate = me + 1 - 2 * core
    mine = me // 2
    own_half = mine // hh
    halves = (own_half, 1 - own_half)
    froms = [lax.rem(mine - k + half, half) for k in range(1, half)]
    at_mate = (mate, col)
    at_x = (me, 1 - col)

    def place_of(k, c):
        return ((k // hh) * 2 + c) * hh + lax.rem(k, hh)

    spot = place_of(mine, core)

    def rcopy(src, dst, ss, rs, dev):
        return pltpu.make_async_remote_copy(
            src_ref=src, dst_ref=dst, send_sem=ss, recv_sem=rs,
            device_id=dev, device_id_type=pl.DeviceIdType.MESH)

    def signal(sem, dev):
        pl.semaphore_signal(sem, inc=1, device_id=dev, device_id_type=pl.DeviceIdType.MESH)

    def at_peer(k):
        return (2 * k + core, col)

    near = hh
    later = [(2, mine == 0), (1, (mine == 0) | (mine == 2))]
    later += [(k, mine < k) for k in range(3, near)]
    earlier = [(0, mine > 0), (2, (mine == 1) | (mine > 2)), (1, mine > 2)]
    earlier += [(k, mine > k) for k in range(3, near)]

    def each(pairs, fn):
        for k, cond in pairs:
            pl.when(cond)(functools.partial(fn, k))

    far_later = [(k, mine < k) for k in range(near, half)]
    far_earlier = [(k, mine > k) for k in range(near, half - 1)]
    n_earlier = jnp.where(mine == 1, 2, jnp.where(mine == 2, 1, mine))
    n_far = jnp.where(mine < near, half - near, half - 1 - mine)

    barrier = pltpu.get_barrier_semaphore()
    pl.when(col == 0)(lambda: signal(barrier, at_x))
    signal(barrier, at_mate)
    each(later, lambda k: signal(barrier, at_peer(k)))
    each(far_later, lambda k: signal(barrier, at_peer(k)))

    small = []
    step = q_w * btiles
    loads = [pltpu.make_async_copy(
        cnt_hbm.at[pl.ds(q * step, step), :], cnt_v.at[pl.ds(q * step, step), :], dsem.at[q])
        for q in range(nq)]
    loads[0].start()
    for k, (src, dst) in enumerate(((cm_hbm, cm_ref), (c_hbm, c_ref), (occ_hbm, occ_ref),
                                    (rm_hbm, rm_ref))):
        cp = pltpu.make_async_copy(src, dst, dsem.at[nq + 1 + k])
        cp.start()
        small.append(cp)
    for cp in loads[1:]:
        cp.start()
    rload = pltpu.make_async_copy(r_hbm, r_v, dsem.at[nq])

    pl.semaphore_wait(barrier, 1 + col + n_earlier)
    slot = jnp.minimum(mine, near)
    pl.when(col == 1)(lambda: signal(x_token, at_x))
    each(earlier, lambda k: signal(token.at[slot], at_peer(k)))
    each(far_earlier, lambda k: signal(token.at[slot], at_peer(k)))

    for cp in small:
        cp.wait()

    log_c = jnp.log(cm_ref[...].astype(jnp.float32))
    ri = lax.broadcasted_iota(jnp.int32, (w, w), 0)
    ci = lax.broadcasted_iota(jnp.int32, (w, w), 1)
    log_c = jnp.sum(jnp.where(ri == ci, jnp.broadcast_to(log_c, (w, w)), 0.0), axis=1, keepdims=True)
    hi, mid, lo = split3(log_c)
    blk[...] = jnp.zeros_like(blk)
    blk[:, pl.ds(0, d)] = c_ref[...].astype(jnp.float32)
    li = lax.broadcasted_iota(jnp.int32, (w, dp), 1)
    own = blk[...]
    for at, val in ((d, hi), (d + 1, mid), (d + 2, lo)):
        own = jnp.where(li == at, val, own)
    own = jnp.where((li >= d + 3) & (li < d + 6), 1.0, own)
    cg[0, spot] = own.astype(jnp.bfloat16)

    ident = eye(LANES)

    def codes(q):
        loads[q].wait()
        for t in range(btiles):
            cells = []
            for u in range(q_w // tile):
                x = cnt_v[pl.ds(q * step + u * tile * btiles + t, tile, stride=btiles), :]
                k = q * (q_w // tile) + u
                on = jnp.broadcast_to(occ_ref[t:t + 1, k:k + 1], (tile, LANES)) != 0
                cells.append(jnp.where(on, x, -1).astype(jnp.float32).astype(jnp.bfloat16))
            code = nt(ident, jnp.concatenate(cells, axis=0)).astype(jnp.bfloat16)
            for r in range(LANES // w):
                b = t * (LANES // w) + r
                k = b // 2
                at = pl.ds((((k // hh) * 2 + b % 2) * hh + k % hh) * w, w)
                enc[0, q, at, :] = code[r * w:(r + 1) * w]

    def slopes(q):
        def one(s):
            at = pl.ds(s * sub, sub)
            slope_v[q, at, :], logc_v[q, at, :] = slope_terms(enc[0, q, at, :].astype(jnp.float32))

        repeat(nsub, one)

    def encode(q):
        codes(q)
        slopes(q)

    def x_start(q, part):
        at = pl.ds(pl.multiple_of(part * gcols, gcols), gcols)
        rcopy(enc.at[0, q, at], enc.at[1, q, at], e_s, e_r.at[q], at_x).start()

    def x_starts(q):
        x_start(q, 0)
        x_start(q, 1)

    ecopies = [rcopy(enc.at[0, q], enc.at[1, q], e_s, e_r.at[q], at_x) for q in range(nq)]
    xcp = rcopy(cg.at[0, spot], cg.at[1, spot], gx_s, gx_r, at_x)

    def to_near(which, waiting):
        def one(k):
            if waiting:
                pl.semaphore_wait(token.at[k], 1)
            if k == 2:
                rcopy(cg.at[which, spot], cg.at[which, spot], g_s, w_r.at[which],
                      at_peer(k)).start()
            else:
                direct(which, k)

        each(later, one)

    def direct(which, k):
        rcopy(cg.at[which, spot], cg.at[which, spot], g_s, g_r.at[which, own_half],
              at_peer(k)).start()

    def to_earlier(which):
        each(earlier, functools.partial(direct, which))
        each(far_earlier, functools.partial(direct, which))

    def to_far(which):
        for k, cond in far_later:
            pl.when(cond & (mine > 0))(functools.partial(direct, which, k))

    def far_ready():
        @pl.when(n_far > 0)
        def _():
            pl.semaphore_wait(token.at[near], n_far)

    def relay(which):
        @pl.when(mine == 2)
        def _():
            at = cg.at[which, place_of(0, core)]
            rcopy(at, at, w_s, w_r.at[which], at_mate).wait_recv()
            for k in range(near, half):
                if which:
                    rcopy(at, at, w_s, g_r.at[which, 0], at_peer(k)).start()
                else:
                    for c in range(2):
                        rcopy(at, at, w_s, w_r.at[which], (2 * k + c, col)).start()

    to_earlier(0)
    codes(0)

    def cross():
        pl.when(col == 0)(lambda: pl.semaphore_wait(x_token, 1))
        xcp.start()
        x_starts(0)

    first = (col == 1) | (mine < near)
    pl.when(first)(cross)

    @pl.when(mine >= near)
    def _():
        far_ready()
        to_far(0)

    pl.when(jnp.logical_not(first))(cross)
    slopes(0)
    if nq > 2:
        encode(1)
    to_near(0, True)
    pl.when((mine > 0) & (mine < near))(far_ready)
    relay(0)
    pl.when(mine < near)(lambda: to_far(0))
    rload.start()
    for q in range(2, nq):
        x_starts(q - 1)
        encode(q)

    rload.wait()
    raug[pl.ds(0, d), :] = r_v[...]
    base = (d // 16) * 16
    row_term = jnp.log(rm_ref[...].astype(jnp.float32)) - lt_ref[0]
    hi, mid, lo = split3(row_term)
    tail = raug[pl.ds(base, dp - base), :].astype(jnp.float32)
    si = lax.broadcasted_iota(jnp.int32, (dp - base, rows), 0) + base
    tail = jnp.where(si < d, tail, jnp.where(si < d + 3, 1.0, 0.0))
    for at, val in ((d + 3, hi), (d + 4, mid), (d + 5, lo)):
        tail = jnp.where(si == at, val, tail)
    raug[pl.ds(base, dp - base), :] = tail.astype(jnp.bfloat16)

    def arrived(which, h, blocks):
        some = cg.at[which, pl.ds(0, blocks)]
        rcopy(some, some, g_s, g_r.at[which, h], at_mate).wait_recv()

    def to_mate(which, h, skip):
        part = cg.at[which, pl.ds((h * 2 + core) * hh + skip, hh - skip)]
        return rcopy(part, part, m_s, m_r.at[which, h], at_mate)

    def gathered(which, at):
        h = halves[at]

        def took(blocks, skip):
            arrived(which, h, blocks)
            to_mate(which, h, skip).start()

        if at and which:
            took(hh, 0)
        elif at:
            pl.when(mine < hh)(lambda: took(hh, 0))
            pl.when(mine >= hh)(lambda: took(hh - 1, 1))
        else:
            pl.when(mine == 2)(lambda: took(hh - 2, 0))
            pl.when(mine != 2)(lambda: took(hh - 1, 0))

    def from_mate_blocks(which, at):
        h = halves[at]
        if at and not which:
            pl.when(mine < hh)(lambda: to_mate(which, h, 0).wait_recv())
            pl.when(mine >= hh)(lambda: to_mate(which, h, 1).wait_recv())
        else:
            to_mate(which, h, 0).wait_recv()

    def first_chip():
        two = cg.at[0, pl.ds(0, 2)]
        rcopy(two, two, w_s, w_r.at[0], at_mate).wait_recv()
        ends = (pl.ds(0, w), pl.ds(hh * w, w))

        def both(fn):
            return jnp.concatenate([fn(at) for at in ends], axis=0)

        blocks = jnp.concatenate([cg[0, 0], cg[0, hh]], axis=0)
        for q in range(nq):
            qs = pl.ds(q * q_w, q_w)
            gap = nn(blocks, raug[:, qs])
            code = both(lambda at: enc[0, q, at, :]).astype(jnp.float32)
            slope = both(lambda at: slope_v[q, at, :])
            logc = both(lambda at: logc_v[q, at, :])
            res0[:, qs] = cell(code, slope, logc, gap).astype(jnp.bfloat16)
        s0src[...] = nt(res0[...], raug[...]).reshape(2, w, dp).astype(jnp.bfloat16)
        spare = (mine - hh) * 2 + core
        for c in range(2):
            rcopy(s0src.at[c], s0buf.at[spare], c_s, c_r, (c, col)).start()

    def block(which, first, count):
        return cg[which, pl.ds(first, count)].reshape(count * w, dp)

    def reduced(k):
        return rcopy(s2src.at[k], s2buf.at[mine], b_s, b_r, at_peer(k))

    def from_mate(h):
        return rcopy(gcol.at[pl.ds((h * 2 + 1 - core) * hh, hh)], s1buf.at[pl.ds(h * hh, hh)],
                     a_s, a_r.at[h], at_mate)

    def half_terms(h):
        for q in range(nq):
            qs = pl.ds(q * q_w, q_w)

            def cells(s):
                at = pl.ds(pl.multiple_of(h * gcols + s * subg, subg), subg)
                gap = nn(block(0, (h * gcols + s * subg) // w, subg // w), raug[:, qs])
                code = enc[0, q, at, :].astype(jnp.float32)
                got = cell(code, slope_v[q, at, :], logc_v[q, at, :], gap).astype(jnp.bfloat16)
                res[at, qs] = got
                if q == nq - 1:
                    enc[0, q, at, :] = got

            repeat(nsubg, cells)

        def terms(s):
            at = pl.ds(pl.multiple_of(h * gcols + s * subg, subg), subg)
            part = nt(res[at, :], raug[...]).reshape(subg // w, w, dp)
            gcol[pl.ds((h * gcols + s * subg) // w, subg // w)] = part

        repeat(nsubg, terms)

    def spread(h, own):
        from_mate(h).wait_recv()
        for i in range(hh):
            k = h * hh + i
            total = gcol[(h * 2 + core) * hh + i] + s1buf[k]
            s2src[k] = total.astype(s2src.dtype)
            if own:
                @pl.when(mine == k)
                def _():
                    blk[...] = total

            if i and own:
                pl.when(mine != k - 1)(lambda: reduced(k - 1).start())
            elif i == 1:
                pl.when(mine < hh)(lambda: reduced(k - 1).start())
            elif i:
                reduced(k - 1).start()

    def spread_last(h, own):
        k = h * hh + hh - 1
        if own:
            pl.when(mine != k)(lambda: reduced(k).start())
        else:
            reduced(k).start()

    ident_d = eye(dp)

    def transposed(which, h):
        def one(s):
            part = block(which, (h * gcols + s * subg) // w, subg // w)
            at = pl.ds(pl.multiple_of(h * gcols + s * subg, subg), subg)
            cd[which, :, at] = nt(ident_d, part).astype(jnp.bfloat16)

        repeat(nsubg, one)

    def other_cells(q, h):
        qs = pl.ds(q * q_w, q_w)

        def cells(s):
            at = pl.ds(pl.multiple_of(h * gcols + s * subg, subg), subg)
            gap = nn(block(1, (h * gcols + s * subg) // w, subg // w), raug[:, qs])
            code = enc[1, q, at, :].astype(jnp.float32)
            slope, logc = slope_terms(code)
            enc[1, q, at, :] = cell(code, slope, logc, gap).astype(jnp.bfloat16)

        repeat(nsubg, cells)

    def other_rows(q):
        qs = pl.ds(q * q_w, q_w)
        more = nn(cd[1, :dq, :], enc[1, q])[:d, :]
        rows_out[:, qs] = (rows_out[:, qs] + more) * scale_r

    xcp.wait_recv()
    to_earlier(1)
    to_near(1, False)
    gathered(0, 0)
    from_mate_blocks(0, 0)
    half_terms(own_half)
    from_mate(own_half).start()
    x_start(nq - 1, own_half)
    pl.when(mine >= hh)(first_chip)
    to_far(1)
    gathered(0, 1)
    relay(1)
    from_mate_blocks(0, 1)
    half_terms(1 - own_half)
    pl.when(mine == 0)(far_ready)
    from_mate(1 - own_half).start()
    x_start(nq - 1, 1 - own_half)
    spread(own_half, True)
    transposed(0, 0)
    spread_last(own_half, True)
    spread(1 - own_half, False)
    transposed(0, 1)
    spread_last(1 - own_half, False)
    gathered(1, 0)
    rows_out[...] = nn(cd[0, :dq, :], res[...])[:d, :]

    from_mate_blocks(1, 0)
    transposed(1, own_half)
    sooner = nq // 2
    for q in range(sooner):
        ecopies[q].wait_recv()
        other_cells(q, own_half)
    gathered(1, 1)
    from_mate_blocks(1, 1)
    transposed(1, 1 - own_half)
    for q in range(sooner):
        other_cells(q, 1 - own_half)
        other_rows(q)
    for q in range(sooner, nq):
        ecopies[q].wait_recv()
        if q < nq - 1:
            other_cells(q, 0)
            other_cells(q, 1)
        other_rows(q)

    def summed(blocks):
        got = s2buf.at[pl.ds(0, blocks)]
        return rcopy(got, got, b_s, b_r, at_mate)

    @pl.when(mine == 0)
    def _():
        summed(hh - 1).wait_recv()
        total = blk[...]
        for k in range(1, hh):
            total = total + s2buf[k].astype(jnp.float32)
        rcopy(s0buf, s0buf, c_s, c_r, at_mate).wait_recv()
        for k in range(half):
            total = total + s0buf[k].astype(jnp.float32)
        cols_out[...] = (total * scale_c)[:, :d]

    @pl.when(mine != 0)
    def _():
        summed(half - 1).wait_recv()
        total = blk[...]
        for k in froms:
            total = total + s2buf[k].astype(jnp.float32)
        cols_out[...] = (total * scale_c)[:, :d]

    def sent(blocks):
        some = gcol.at[pl.ds(0, blocks)]
        rcopy(some, some, g_s, gx_r, at_mate).wait_send()

    pl.when(mine == 0)(lambda: sent(near - 1))
    pl.when(mine != 0)(lambda: sent(half - 1))

    @pl.when(mine == 2)
    def _():
        some = gcol.at[pl.ds(0, 3 * (half - near) // 2)]
        rcopy(some, some, w_s, gx_r, at_mate).wait_send()

    xcp.wait_send()
    def told(blocks):
        some = cg.at[0, pl.ds(0, blocks)]
        rcopy(some, some, m_s, gx_r, at_mate).wait_send()

    pl.when(mine < hh)(lambda: told(n))
    pl.when(mine >= hh)(lambda: told(n - 1))
    rcopy(enc.at[0], enc.at[1], e_s, gx_r, at_x).wait_send()
    some = gcol.at[pl.ds(0, half)]
    rcopy(some, some, a_s, gx_r, at_mate).wait_send()
    pl.when(mine < hh)(lambda: summed(half - 1).wait_send())

    @pl.when(mine >= hh)
    def _():
        summed(half - 2).wait_send()
        rcopy(s0src, s0src, c_s, c_r, at_mate).wait_send()


def scratch_bytes(shapes):
    return sum(math.prod(s.shape) * jnp.dtype(s.dtype).itemsize for s in shapes)


def place(rows_in, cols_in, rows_out, cols_out, sem):
    copies = [pltpu.make_async_copy(rows_in, rows_out, sem.at[0]),
              pltpu.make_async_copy(cols_in, cols_out, sem.at[1])]
    for cp in copies:
        cp.start()
    for cp in copies:
        cp.wait()


def body(row_embed, col_embed, counts, occupancy, row_marg, col_marg, log_total):
    n = lax.axis_size("row")
    d, rows = row_embed.shape
    w = col_embed.shape[2]
    band = counts.shape[2]
    tile = rows // occupancy.shape[0]
    q_w = 2 * tile if rows % (2 * tile) == 0 else tile
    dp = -(-(d + 6) // LANES) * LANES
    half = n // 2
    nq = rows // q_w
    btiles = band // LANES
    cfg = (n, d, dp, w, band, rows, tile, q_w,
           1.0 / math.sqrt(w * n * lax.axis_size("col")), 1.0 / math.sqrt(rows * n))
    bf, f32 = jnp.bfloat16, jnp.float32
    vm, hb, anywhere = (pl.BlockSpec(memory_space=m) for m in (pltpu.VMEM, pltpu.HBM, pl.ANY))
    dma = lambda *s: pltpu.SemaphoreType.DMA(s) if s else pltpu.SemaphoreType.DMA
    scratch = [
        pltpu.VMEM((d, rows), bf),
        pltpu.VMEM((rows * btiles, LANES), jnp.int32),
        pltpu.VMEM((dp, rows), bf),
        pltpu.VMEM((w, dp), f32),
        pltpu.VMEM((2, n, w, dp), bf),
        pltpu.VMEM((2, dp, band), bf),
        pltpu.VMEM((2, nq, band, q_w), bf),
        pltpu.VMEM((nq, band, q_w), f32),
        pltpu.VMEM((nq, band, q_w), f32),
        pltpu.VMEM((band, rows), bf),
        pltpu.VMEM((n, w, dp), f32),
        pltpu.VMEM((half, w, dp), f32),
        pltpu.VMEM((half, w, dp), SEND),
        pltpu.VMEM((half, w, dp), SEND),
        pltpu.VMEM((w, d), bf),
        pltpu.VMEM((occupancy.shape[2], occupancy.shape[0]), jnp.int32),
        pltpu.VMEM((1, rows), jnp.int32),
        pltpu.VMEM((1, w), jnp.int32),
        dma(nq + 5),
        dma(), dma(nq), dma(), dma(), dma(), dma(2, 2), dma(), dma(2), dma(), dma(2, 2),
        dma(), dma(2), dma(), dma(),
        pltpu.SemaphoreType.REGULAR((half // 2 + 1,)),
        pltpu.SemaphoreType.REGULAR,
        dma(), dma(),
        pltpu.VMEM((2, w, dp), bf),
        pltpu.VMEM((half, w, dp), bf),
        pltpu.VMEM((2 * w, rows), bf),
    ]
    limit = min(60 << 20, (6 << 20) + scratch_bytes(scratch[:18]) + 2 * d * rows * 4 + 28 * band * q_w)
    grad_rows, grad_cols = pl.pallas_call(
        functools.partial(kernel, cfg),
        out_shape=(jax.ShapeDtypeStruct((d, rows), f32), jax.ShapeDtypeStruct((w, d), f32)),
        in_specs=[hb] * 6 + [pl.BlockSpec(memory_space=pltpu.SMEM)],
        out_specs=(vm, vm),
        scratch_shapes=scratch,
        compiler_params=pltpu.CompilerParams(
            collective_id=0, has_side_effects=True, vmem_limit_bytes=limit),
    )(
        *(pltpu.with_memory_space_constraint(x, pltpu.HBM) for x in (
            row_embed,
            jnp.transpose(col_embed, (1, 2, 0)).reshape(w, d),
            counts.reshape(rows * btiles, LANES),
            jnp.transpose(occupancy, (1, 2, 0)).reshape(occupancy.shape[2], occupancy.shape[0]),
            row_marg.reshape(1, rows),
            col_marg,
        )),
        log_total,
    )
    grad_rows, grad_cols = pl.pallas_call(
        place,
        out_shape=(jax.ShapeDtypeStruct((d, rows), f32), jax.ShapeDtypeStruct((w, d), f32)),
        in_specs=[anywhere, anywhere],
        out_specs=(hb, hb),
        scratch_shapes=[pltpu.SemaphoreType.DMA((2,))],
    )(*(pltpu.with_memory_space_constraint(x, pltpu.VMEM) for x in (grad_rows, grad_cols)))
    return grad_rows, jnp.transpose(grad_cols.reshape(1, w, d), (2, 0, 1))


def solution(mesh):
    placed = (
        P(None, "row"),
        P(None, "col", "row"),
        P("row", "col", None),
        P("row", "col", None),
        P("row"),
        P("col", "row"),
        P(),
    )
    return jax.shard_map(
        body,
        mesh=mesh,
        in_specs=placed,
        out_specs=(P(None, "row"), P(None, "col", "row")),
        check_vma=False,
    )
```

```python
import functools
import math

import jax
import jax.numpy as jnp
from jax import lax
from jax.experimental import pallas as pl
from jax.experimental.pallas import tpu as pltpu
from jax.sharding import PartitionSpec as P

LANES = 128
SEND = jnp.bfloat16


def nt(a, b):
    return lax.dot_general(a, b, (((1,), (1,)), ((), ())), preferred_element_type=jnp.float32)


def nn(a, b):
    return lax.dot_general(a, b, (((1,), (0,)), ((), ())), preferred_element_type=jnp.float32)


def split3(x):
    hi = x.astype(jnp.bfloat16).astype(jnp.float32)
    rest = x - hi
    mid = rest.astype(jnp.bfloat16).astype(jnp.float32)
    return hi, mid, rest - mid


def eye(n):
    r = lax.broadcasted_iota(jnp.int32, (n, n), 0)
    c = lax.broadcasted_iota(jnp.int32, (n, n), 1)
    return (r == c).astype(jnp.float32).astype(jnp.bfloat16)


def slope_terms(code):
    slope = jnp.where(code > 0.0, 0.1 + 0.25 * jnp.sqrt(jnp.maximum(code, 0.0)), 0.0)
    return slope, jnp.log(jnp.maximum(code, 1.0))


def cell(code, slope, logc, gap):
    return jnp.where(code == 0.0, jax.nn.sigmoid(gap), slope * (gap - logc))


def repeat(n, fn):
    if n == 1:
        fn(0)
    else:
        pl.loop(0, n)(fn)


def kernel(cfg, r_hbm, c_hbm, cnt_hbm, occ_hbm, rm_hbm, cm_hbm, lt_ref,
           rows_out, cols_out, cd1, last,
           r_v, cnt_v, raug, blk, cg, cd0, enc, slope_v, logc_v, res, gcol, s1buf, s2src, s2buf,
           c_ref, occ_ref, rm_ref, cm_ref, dsem, e_s, e_r, gx_s, gx_r, g_s, g_r, w_s, w_r, m_s, m_r,
           a_s, a_r, b_s, b_r, token, x_token, c_s, c_r, s0src, s0buf, res0):
    n, d, dp, w, band, rows, tile, q_w, scale_r, scale_c = cfg
    half = n // 2
    dq = -(-d // 16) * 16
    hh = half // 2
    nq = rows // q_w
    btiles = band // LANES
    sub = min(band, 256)
    nsub = band // sub
    gcols = band // 2
    subg = min(gcols, 256)
    nsubg = gcols // subg
    me = lax.axis_index("row")
    col = lax.axis_index("col")
    core = lax.rem(me, 2)
    mate = me + 1 - 2 * core
    mine = me // 2
    own_half = mine // hh
    halves = (own_half, 1 - own_half)
    froms = [lax.rem(mine - k + half, half) for k in range(1, half)]
    at_mate = (mate, col)
    at_x = (me, 1 - col)

    def place_of(k, c):
        return ((k // hh) * 2 + c) * hh + lax.rem(k, hh)

    spot = place_of(mine, core)

    def rcopy(src, dst, ss, rs, dev):
        return pltpu.make_async_remote_copy(
            src_ref=src, dst_ref=dst, send_sem=ss, recv_sem=rs,
            device_id=dev, device_id_type=pl.DeviceIdType.MESH)

    def signal(sem, dev):
        pl.semaphore_signal(sem, inc=1, device_id=dev, device_id_type=pl.DeviceIdType.MESH)

    def at_peer(k):
        return (2 * k + core, col)

    near = hh
    later = [(2, mine == 0), (1, (mine == 0) | (mine == 2))]
    later += [(k, mine < k) for k in range(3, near)]
    earlier = [(0, mine > 0), (2, (mine == 1) | (mine > 2)), (1, mine > 2)]
    earlier += [(k, mine > k) for k in range(3, near)]

    def each(pairs, fn):
        for k, cond in pairs:
            pl.when(cond)(functools.partial(fn, k))

    far_later = [(k, mine < k) for k in range(near, half)]
    far_earlier = [(k, mine > k) for k in range(near, half - 1)]
    n_earlier = jnp.where(mine == 1, 2, jnp.where(mine == 2, 1, mine))
    n_far = jnp.where(mine < near, half - near, half - 1 - mine)

    barrier = pltpu.get_barrier_semaphore()
    pl.when(col == 0)(lambda: signal(barrier, at_x))
    signal(barrier, at_mate)
    each(later, lambda k: signal(barrier, at_peer(k)))
    each(far_later, lambda k: signal(barrier, at_peer(k)))

    small = []
    step = q_w * btiles
    loads = [pltpu.make_async_copy(
        cnt_hbm.at[pl.ds(q * step, step), :], cnt_v.at[pl.ds(q * step, step), :], dsem.at[q])
        for q in range(nq)]
    loads[0].start()
    for k, (src, dst) in enumerate(((cm_hbm, cm_ref), (c_hbm, c_ref), (occ_hbm, occ_ref),
                                    (rm_hbm, rm_ref))):
        cp = pltpu.make_async_copy(src, dst, dsem.at[nq + 1 + k])
        cp.start()
        small.append(cp)
    for cp in loads[1:]:
        cp.start()
    rload = pltpu.make_async_copy(r_hbm, r_v, dsem.at[nq])

    pl.semaphore_wait(barrier, 1 + col + n_earlier)
    slot = jnp.minimum(mine, near)
    pl.when(col == 1)(lambda: signal(x_token, at_x))
    each(earlier, lambda k: signal(token.at[slot], at_peer(k)))
    each(far_earlier, lambda k: signal(token.at[slot], at_peer(k)))

    for cp in small:
        cp.wait()

    log_c = jnp.log(cm_ref[...].astype(jnp.float32))
    ri = lax.broadcasted_iota(jnp.int32, (w, w), 0)
    ci = lax.broadcasted_iota(jnp.int32, (w, w), 1)
    log_c = jnp.sum(jnp.where(ri == ci, jnp.broadcast_to(log_c, (w, w)), 0.0), axis=1, keepdims=True)
    hi, mid, lo = split3(log_c)
    blk[...] = jnp.zeros_like(blk)
    blk[:, pl.ds(0, d)] = c_ref[...].astype(jnp.float32)
    li = lax.broadcasted_iota(jnp.int32, (w, dp), 1)
    own = blk[...]
    for at, val in ((d, hi), (d + 1, mid), (d + 2, lo)):
        own = jnp.where(li == at, val, own)
    own = jnp.where((li >= d + 3) & (li < d + 6), 1.0, own)
    cg[0, spot] = own.astype(jnp.bfloat16)

    ident = eye(LANES)

    def codes(q):
        loads[q].wait()
        for t in range(btiles):
            cells = []
            for u in range(q_w // tile):
                x = cnt_v[pl.ds(q * step + u * tile * btiles + t, tile, stride=btiles), :]
                k = q * (q_w // tile) + u
                on = jnp.broadcast_to(occ_ref[t:t + 1, k:k + 1], (tile, LANES)) != 0
                cells.append(jnp.where(on, x, -1).astype(jnp.float32).astype(jnp.bfloat16))
            code = nt(ident, jnp.concatenate(cells, axis=0)).astype(jnp.bfloat16)
            for r in range(LANES // w):
                b = t * (LANES // w) + r
                k = b // 2
                at = pl.ds((((k // hh) * 2 + b % 2) * hh + k % hh) * w, w)
                enc[0, q, at, :] = code[r * w:(r + 1) * w]

    def slopes(q):
        def one(s):
            at = pl.ds(s * sub, sub)
            slope_v[q, at, :], logc_v[q, at, :] = slope_terms(enc[0, q, at, :].astype(jnp.float32))

        repeat(nsub, one)

    def encode(q):
        codes(q)
        slopes(q)

    def x_start(q, part):
        at = pl.ds(pl.multiple_of(part * gcols, gcols), gcols)
        rcopy(enc.at[0, q, at], enc.at[1, q, at], e_s, e_r.at[q], at_x).start()

    def x_starts(q):
        x_start(q, 0)
        x_start(q, 1)

    ecopies = [rcopy(enc.at[0, q], enc.at[1, q], e_s, e_r.at[q], at_x) for q in range(nq)]
    xcp = rcopy(cg.at[0, spot], cg.at[1, spot], gx_s, gx_r, at_x)

    def to_near(which, waiting):
        def one(k):
            if waiting:
                pl.semaphore_wait(token.at[k], 1)
            if k == 2:
                rcopy(cg.at[which, spot], cg.at[which, spot], g_s, w_r.at[which],
                      at_peer(k)).start()
            else:
                direct(which, k)

        each(later, one)

    def direct(which, k):
        rcopy(cg.at[which, spot], cg.at[which, spot], g_s, g_r.at[which, own_half],
              at_peer(k)).start()

    def to_earlier(which):
        each(earlier, functools.partial(direct, which))
        each(far_earlier, functools.partial(direct, which))

    def to_far(which):
        for k, cond in far_later:
            pl.when(cond & (mine > 0))(functools.partial(direct, which, k))

    def far_ready():
        @pl.when(n_far > 0)
        def _():
            pl.semaphore_wait(token.at[near], n_far)

    def relay(which):
        @pl.when(mine == 2)
        def _():
            at = cg.at[which, place_of(0, core)]
            rcopy(at, at, w_s, w_r.at[which], at_mate).wait_recv()
            for k in range(near, half):
                if which:
                    rcopy(at, at, w_s, g_r.at[which, 0], at_peer(k)).start()
                else:
                    for c in range(2):
                        rcopy(at, at, w_s, w_r.at[which], (2 * k + c, col)).start()

    to_earlier(0)
    codes(0)

    def cross():
        pl.when(col == 0)(lambda: pl.semaphore_wait(x_token, 1))
        xcp.start()
        x_starts(0)

    first = (col == 1) | (mine < near)
    pl.when(first)(cross)

    @pl.when(mine >= near)
    def _():
        far_ready()
        to_far(0)

    pl.when(jnp.logical_not(first))(cross)
    slopes(0)
    if nq > 2:
        encode(1)
    to_near(0, True)
    pl.when((mine > 0) & (mine < near))(far_ready)
    relay(0)
    pl.when(mine < near)(lambda: to_far(0))
    rload.start()
    for q in range(2, nq):
        x_starts(q - 1)
        encode(q)

    rload.wait()
    raug[pl.ds(0, d), :] = r_v[...]
    base = (d // 16) * 16
    row_term = jnp.log(rm_ref[...].astype(jnp.float32)) - lt_ref[0]
    hi, mid, lo = split3(row_term)
    tail = raug[pl.ds(base, dp - base), :].astype(jnp.float32)
    si = lax.broadcasted_iota(jnp.int32, (dp - base, rows), 0) + base
    tail = jnp.where(si < d, tail, jnp.where(si < d + 3, 1.0, 0.0))
    for at, val in ((d + 3, hi), (d + 4, mid), (d + 5, lo)):
        tail = jnp.where(si == at, val, tail)
    raug[pl.ds(base, dp - base), :] = tail.astype(jnp.bfloat16)

    def arrived(which, h, blocks):
        some = cg.at[which, pl.ds(0, blocks)]
        rcopy(some, some, g_s, g_r.at[which, h], at_mate).wait_recv()

    def to_mate(which, h, skip):
        part = cg.at[which, pl.ds((h * 2 + core) * hh + skip, hh - skip)]
        return rcopy(part, part, m_s, m_r.at[which, h], at_mate)

    def gathered(which, at):
        h = halves[at]

        def took(blocks, skip):
            arrived(which, h, blocks)
            to_mate(which, h, skip).start()

        if at and which:
            took(hh, 0)
        elif at:
            pl.when(mine < hh)(lambda: took(hh, 0))
            pl.when(mine >= hh)(lambda: took(hh - 1, 1))
        else:
            pl.when(mine == 2)(lambda: took(hh - 2, 0))
            pl.when(mine != 2)(lambda: took(hh - 1, 0))

    def from_mate_blocks(which, at):
        h = halves[at]
        if at and not which:
            pl.when(mine < hh)(lambda: to_mate(which, h, 0).wait_recv())
            pl.when(mine >= hh)(lambda: to_mate(which, h, 1).wait_recv())
        else:
            to_mate(which, h, 0).wait_recv()

    def first_chip():
        two = cg.at[0, pl.ds(0, 2)]
        rcopy(two, two, w_s, w_r.at[0], at_mate).wait_recv()
        ends = (pl.ds(0, w), pl.ds(hh * w, w))

        def both(fn):
            return jnp.concatenate([fn(at) for at in ends], axis=0)

        blocks = jnp.concatenate([cg[0, 0], cg[0, hh]], axis=0)
        for q in range(nq):
            qs = pl.ds(q * q_w, q_w)
            gap = nn(blocks, raug[:, qs])
            code = both(lambda at: enc[0, q, at, :]).astype(jnp.float32)
            slope = both(lambda at: slope_v[q, at, :])
            logc = both(lambda at: logc_v[q, at, :])
            res0[:, qs] = cell(code, slope, logc, gap).astype(jnp.bfloat16)
        s0src[...] = nt(res0[...], raug[...]).reshape(2, w, dp).astype(jnp.bfloat16)
        spare = (mine - hh) * 2 + core
        for c in range(2):
            rcopy(s0src.at[c], s0buf.at[spare], c_s, c_r, (c, col)).start()

    def block(which, first, count):
        return cg[which, pl.ds(first, count)].reshape(count * w, dp)

    def reduced(k):
        return rcopy(s2src.at[k], s2buf.at[mine], b_s, b_r, at_peer(k))

    def from_mate(h):
        return rcopy(gcol.at[pl.ds((h * 2 + 1 - core) * hh, hh)], s1buf.at[pl.ds(h * hh, hh)],
                     a_s, a_r.at[h], at_mate)

    def half_terms(h):
        for q in range(nq):
            qs = pl.ds(q * q_w, q_w)

            def cells(s):
                at = pl.ds(pl.multiple_of(h * gcols + s * subg, subg), subg)
                gap = nn(block(0, (h * gcols + s * subg) // w, subg // w), raug[:, qs])
                code = enc[0, q, at, :].astype(jnp.float32)
                got = cell(code, slope_v[q, at, :], logc_v[q, at, :], gap).astype(jnp.bfloat16)
                res[at, qs] = got
                if q == nq - 1:
                    enc[0, q, at, :] = got

            repeat(nsubg, cells)

        def terms(s):
            at = pl.ds(pl.multiple_of(h * gcols + s * subg, subg), subg)
            part = nt(res[at, :], raug[...]).reshape(subg // w, w, dp)
            gcol[pl.ds((h * gcols + s * subg) // w, subg // w)] = part

        repeat(nsubg, terms)

    def spread(h, own):
        from_mate(h).wait_recv()
        for i in range(hh):
            k = h * hh + i
            total = gcol[(h * 2 + core) * hh + i] + s1buf[k]
            s2src[k] = total.astype(s2src.dtype)
            if own:
                @pl.when(mine == k)
                def _():
                    blk[...] = total

            if i and own:
                pl.when(mine != k - 1)(lambda: reduced(k - 1).start())
            elif i == 1:
                pl.when(mine < hh)(lambda: reduced(k - 1).start())
            elif i:
                reduced(k - 1).start()

    def spread_last(h, own):
        k = h * hh + hh - 1
        if own:
            pl.when(mine != k)(lambda: reduced(k).start())
        else:
            reduced(k).start()

    ident_d = eye(dp)

    def transposed(which, h):
        def one(s):
            part = block(which, (h * gcols + s * subg) // w, subg // w)
            at = pl.ds(pl.multiple_of(h * gcols + s * subg, subg), subg)
            (cd1 if which else cd0)[:, at] = nt(ident_d, part)[:dq, :].astype(jnp.bfloat16)

        repeat(nsubg, one)

    def other_cells(q, h):
        qs = pl.ds(q * q_w, q_w)

        def cells(s):
            at = pl.ds(pl.multiple_of(h * gcols + s * subg, subg), subg)
            gap = nn(block(1, (h * gcols + s * subg) // w, subg // w), raug[:, qs])
            code = enc[1, q, at, :].astype(jnp.float32)
            slope, logc = slope_terms(code)
            enc[1, q, at, :] = cell(code, slope, logc, gap).astype(jnp.bfloat16)

        repeat(nsubg, cells)

    def other_rows(q):
        qs = pl.ds(q * q_w, q_w)
        more = nn(cd1[...], enc[1, q])[:d, :]
        rows_out[:, qs] = (rows_out[:, qs] + more) * scale_r

    xcp.wait_recv()
    to_earlier(1)
    to_near(1, False)
    gathered(0, 0)
    from_mate_blocks(0, 0)
    half_terms(own_half)
    from_mate(own_half).start()
    x_start(nq - 1, own_half)
    pl.when(mine >= hh)(first_chip)
    to_far(1)
    gathered(0, 1)
    relay(1)
    from_mate_blocks(0, 1)
    half_terms(1 - own_half)
    pl.when(mine == 0)(far_ready)
    from_mate(1 - own_half).start()
    x_start(nq - 1, 1 - own_half)
    spread(own_half, True)
    transposed(0, 0)
    spread_last(own_half, True)
    spread(1 - own_half, False)
    transposed(0, 1)
    spread_last(1 - own_half, False)
    gathered(1, 0)
    rows_out[...] = nn(cd0[...], res[...])[:d, :]

    gathered(1, 1)
    from_mate_blocks(1, 0)
    transposed(1, own_half)
    sooner = nq // 2
    for q in range(sooner):
        ecopies[q].wait_recv()
        other_cells(q, own_half)
    from_mate_blocks(1, 1)
    transposed(1, 1 - own_half)
    for q in range(sooner):
        other_cells(q, 1 - own_half)
        other_rows(q)
    for q in range(sooner, nq):
        ecopies[q].wait_recv()
        if q < nq - 1:
            other_cells(q, 0)
            other_cells(q, 1)
            other_rows(q)
        else:
            last[...] = enc[1, q]

    def summed(blocks):
        got = s2buf.at[pl.ds(0, blocks)]
        return rcopy(got, got, b_s, b_r, at_mate)

    @pl.when(mine == 0)
    def _():
        summed(hh - 1).wait_recv()
        total = blk[...]
        for k in range(1, hh):
            total = total + s2buf[k].astype(jnp.float32)
        rcopy(s0buf, s0buf, c_s, c_r, at_mate).wait_recv()
        for k in range(half):
            total = total + s0buf[k].astype(jnp.float32)
        cols_out[...] = (total * scale_c)[:, :d]

    @pl.when(mine != 0)
    def _():
        summed(half - 1).wait_recv()
        total = blk[...]
        for k in froms:
            total = total + s2buf[k].astype(jnp.float32)
        cols_out[...] = (total * scale_c)[:, :d]

    def sent(blocks):
        some = gcol.at[pl.ds(0, blocks)]
        rcopy(some, some, g_s, gx_r, at_mate).wait_send()

    pl.when(mine == 0)(lambda: sent(near - 1))
    pl.when(mine != 0)(lambda: sent(half - 1))

    @pl.when(mine == 2)
    def _():
        some = gcol.at[pl.ds(0, 3 * (half - near) // 2)]
        rcopy(some, some, w_s, gx_r, at_mate).wait_send()

    xcp.wait_send()
    def told(blocks):
        some = cg.at[0, pl.ds(0, blocks)]
        rcopy(some, some, m_s, gx_r, at_mate).wait_send()

    pl.when(mine < hh)(lambda: told(n))
    pl.when(mine >= hh)(lambda: told(n - 1))
    rcopy(enc.at[0], enc.at[1], e_s, gx_r, at_x).wait_send()
    some = gcol.at[pl.ds(0, half)]
    rcopy(some, some, a_s, gx_r, at_mate).wait_send()
    pl.when(mine < hh)(lambda: summed(half - 1).wait_send())

    @pl.when(mine >= hh)
    def _():
        summed(half - 2).wait_send()
        rcopy(s0src, s0src, c_s, c_r, at_mate).wait_send()


def scratch_bytes(shapes):
    return sum(math.prod(s.shape) * jnp.dtype(s.dtype).itemsize for s in shapes)


def place(scale_r, rows_in, cols_in, cd1, last, rows_out, cols_out, end, sem):
    d, rows = rows_in.shape
    done = rows - last.shape[1]
    copies = [pltpu.make_async_copy(cols_in, cols_out, sem.at[0]),
              pltpu.make_async_copy(rows_in.at[:, pl.ds(0, done)], rows_out.at[:, pl.ds(0, done)], sem.at[1]),
              pltpu.make_async_copy(end, rows_out.at[:, pl.ds(done, rows - done)], sem.at[2])]
    copies[0].start()
    copies[1].start()
    more = nn(cd1[...], last[...])[:d, :]
    end[...] = (rows_in[:, pl.ds(done, rows - done)] + more) * scale_r
    copies[2].start()
    for cp in copies:
        cp.wait()


def body(row_embed, col_embed, counts, occupancy, row_marg, col_marg, log_total):
    n = lax.axis_size("row")
    d, rows = row_embed.shape
    w = col_embed.shape[2]
    band = counts.shape[2]
    tile = rows // occupancy.shape[0]
    q_w = 2 * tile if rows % (2 * tile) == 0 else tile
    dp = -(-(d + 6) // LANES) * LANES
    half = n // 2
    nq = rows // q_w
    dq = -(-d // 16) * 16
    btiles = band // LANES
    cfg = (n, d, dp, w, band, rows, tile, q_w,
           1.0 / math.sqrt(w * n * lax.axis_size("col")), 1.0 / math.sqrt(rows * n))
    bf, f32 = jnp.bfloat16, jnp.float32
    vm, hb, anywhere = (pl.BlockSpec(memory_space=m) for m in (pltpu.VMEM, pltpu.HBM, pl.ANY))
    dma = lambda *s: pltpu.SemaphoreType.DMA(s) if s else pltpu.SemaphoreType.DMA
    scratch = [
        pltpu.VMEM((d, rows), bf),
        pltpu.VMEM((rows * btiles, LANES), jnp.int32),
        pltpu.VMEM((dp, rows), bf),
        pltpu.VMEM((w, dp), f32),
        pltpu.VMEM((2, n, w, dp), bf),
        pltpu.VMEM((dq, band), bf),
        pltpu.VMEM((2, nq, band, q_w), bf),
        pltpu.VMEM((nq, band, q_w), f32),
        pltpu.VMEM((nq, band, q_w), f32),
        pltpu.VMEM((band, rows), bf),
        pltpu.VMEM((n, w, dp), f32),
        pltpu.VMEM((half, w, dp), f32),
        pltpu.VMEM((half, w, dp), SEND),
        pltpu.VMEM((half, w, dp), SEND),
        pltpu.VMEM((w, d), bf),
        pltpu.VMEM((occupancy.shape[2], occupancy.shape[0]), jnp.int32),
        pltpu.VMEM((1, rows), jnp.int32),
        pltpu.VMEM((1, w), jnp.int32),
        dma(nq + 5),
        dma(), dma(nq), dma(), dma(), dma(), dma(2, 2), dma(), dma(2), dma(), dma(2, 2),
        dma(), dma(2), dma(), dma(),
        pltpu.SemaphoreType.REGULAR((half // 2 + 1,)),
        pltpu.SemaphoreType.REGULAR,
        dma(), dma(),
        pltpu.VMEM((2, w, dp), bf),
        pltpu.VMEM((half, w, dp), bf),
        pltpu.VMEM((2 * w, rows), bf),
    ]
    limit = min(60 << 20, (6 << 20) + scratch_bytes(scratch[:18]) + 2 * d * rows * 4 + 28 * band * q_w)
    parts = pl.pallas_call(
        functools.partial(kernel, cfg),
        out_shape=(jax.ShapeDtypeStruct((d, rows), f32), jax.ShapeDtypeStruct((w, d), f32),
                   jax.ShapeDtypeStruct((dq, band), bf), jax.ShapeDtypeStruct((band, q_w), bf)),
        in_specs=[hb] * 6 + [pl.BlockSpec(memory_space=pltpu.SMEM)],
        out_specs=(vm,) * 4,
        scratch_shapes=scratch,
        compiler_params=pltpu.CompilerParams(
            collective_id=0, has_side_effects=True, vmem_limit_bytes=limit),
    )(
        *(pltpu.with_memory_space_constraint(x, pltpu.HBM) for x in (
            row_embed,
            jnp.transpose(col_embed, (1, 2, 0)).reshape(w, d),
            counts.reshape(rows * btiles, LANES),
            jnp.transpose(occupancy, (1, 2, 0)).reshape(occupancy.shape[2], occupancy.shape[0]),
            row_marg.reshape(1, rows),
            col_marg,
        )),
        log_total,
    )
    grad_rows, grad_cols = pl.pallas_call(
        functools.partial(place, cfg[8]),
        out_shape=(jax.ShapeDtypeStruct((d, rows), f32), jax.ShapeDtypeStruct((w, d), f32)),
        in_specs=[vm] * 4,
        out_specs=(hb, hb),
        scratch_shapes=[pltpu.VMEM((d, q_w), f32), pltpu.SemaphoreType.DMA((3,))],
        compiler_params=pltpu.CompilerParams(vmem_limit_bytes=limit),
    )(*(pltpu.with_memory_space_constraint(x, pltpu.VMEM) for x in parts))
    return grad_rows, jnp.transpose(grad_cols.reshape(1, w, d), (2, 0, 1))


def solution(mesh):
    placed = (
        P(None, "row"),
        P(None, "col", "row"),
        P("row", "col", None),
        P("row", "col", None),
        P("row"),
        P("col", "row"),
        P(),
    )
    return jax.shard_map(
        body,
        mesh=mesh,
        in_specs=placed,
        out_specs=(P(None, "row"), P(None, "col", "row")),
        check_vma=False,
    )
```

```python
import functools
import math

import jax
import jax.numpy as jnp
from jax import lax
from jax.experimental import pallas as pl
from jax.experimental.pallas import tpu as pltpu
from jax.sharding import PartitionSpec as P

LANES = 128
SEND = jnp.bfloat16


def nt(a, b):
    return lax.dot_general(a, b, (((1,), (1,)), ((), ())), preferred_element_type=jnp.float32)


def nn(a, b):
    return lax.dot_general(a, b, (((1,), (0,)), ((), ())), preferred_element_type=jnp.float32)


def split3(x):
    hi = x.astype(jnp.bfloat16).astype(jnp.float32)
    rest = x - hi
    mid = rest.astype(jnp.bfloat16).astype(jnp.float32)
    return hi, mid, rest - mid


def eye(n):
    r = lax.broadcasted_iota(jnp.int32, (n, n), 0)
    c = lax.broadcasted_iota(jnp.int32, (n, n), 1)
    return (r == c).astype(jnp.float32).astype(jnp.bfloat16)


def slope_terms(code):
    slope = jnp.where(code > 0.0, 0.1 + 0.25 * jnp.sqrt(jnp.maximum(code, 0.0)), 0.0)
    return slope, jnp.log(jnp.maximum(code, 1.0))


def cell(code, slope, logc, gap):
    return jnp.where(code == 0.0, jax.nn.sigmoid(gap), slope * (gap - logc))


def repeat(n, fn):
    if n == 1:
        fn(0)
    else:
        pl.loop(0, n)(fn)


def kernel(cfg, r_hbm, c_hbm, cnt_hbm, occ_hbm, rm_hbm, cm_hbm, lt_ref,
           rows_out, cols_out, cd1, last,
           r_v, cnt_v, raug, blk, cg, cd0, enc, slope_v, logc_v, res, gcol, s1buf, s2src, s2buf,
           c_ref, occ_ref, rm_ref, cm_ref, dsem, e_s, e_r, gx_s, gx_r, g_s, g_r, w_s, w_r, m_s, m_r,
           a_s, a_r, b_s, b_r, token, x_token, c_s, c_r, h_s, h_r, s0src, s0buf, res0, spare):
    n, d, dp, w, band, rows, tile, q_w, scale_r, scale_c = cfg
    half = n // 2
    dq = -(-d // 16) * 16
    hh = half // 2
    nq = rows // q_w
    btiles = band // LANES
    sub = min(band, 256)
    nsub = band // sub
    gcols = band // 2
    subg = min(gcols, 256)
    nsubg = gcols // subg
    me = lax.axis_index("row")
    col = lax.axis_index("col")
    core = lax.rem(me, 2)
    mate = me + 1 - 2 * core
    mine = me // 2
    own_half = mine // hh
    halves = (own_half, 1 - own_half)
    froms = [lax.rem(mine - k + half, half) for k in range(1, half)]
    at_mate = (mate, col)
    at_x = (me, 1 - col)

    def place_of(k, c):
        return ((k // hh) * 2 + c) * hh + lax.rem(k, hh)

    spot = place_of(mine, core)

    def rcopy(src, dst, ss, rs, dev):
        return pltpu.make_async_remote_copy(
            src_ref=src, dst_ref=dst, send_sem=ss, recv_sem=rs,
            device_id=dev, device_id_type=pl.DeviceIdType.MESH)

    def signal(sem, dev):
        pl.semaphore_signal(sem, inc=1, device_id=dev, device_id_type=pl.DeviceIdType.MESH)

    def at_peer(k):
        return (2 * k + core, col)

    near = hh
    later = [(2, mine == 0), (1, (mine == 0) | (mine == 2))]
    later += [(k, mine < k) for k in range(3, near)]
    earlier = [(0, mine > 0), (2, (mine == 1) | (mine > 2)), (1, mine > 2)]
    earlier += [(k, mine > k) for k in range(3, near)]

    def each(pairs, fn):
        for k, cond in pairs:
            pl.when(cond)(functools.partial(fn, k))

    far_later = [(k, mine < k) for k in range(near, half)]
    far_earlier = [(k, mine > k) for k in range(near, half - 1)]
    n_earlier = jnp.where(mine == 1, 2, jnp.where(mine == 2, 1, mine))
    n_far = jnp.where(mine < near, half - near, half - 1 - mine)

    barrier = pltpu.get_barrier_semaphore()
    pl.when(col == 0)(lambda: signal(barrier, at_x))
    signal(barrier, at_mate)
    each(later, lambda k: signal(barrier, at_peer(k)))
    each(far_later, lambda k: signal(barrier, at_peer(k)))

    small = []
    step = q_w * btiles
    loads = [pltpu.make_async_copy(
        cnt_hbm.at[pl.ds(q * step, step), :], cnt_v.at[pl.ds(q * step, step), :], dsem.at[q])
        for q in range(nq)]
    loads[0].start()
    for k, (src, dst) in enumerate(((cm_hbm, cm_ref), (c_hbm, c_ref), (occ_hbm, occ_ref),
                                    (rm_hbm, rm_ref))):
        cp = pltpu.make_async_copy(src, dst, dsem.at[nq + 1 + k])
        cp.start()
        small.append(cp)
    for cp in loads[1:]:
        cp.start()
    rload = pltpu.make_async_copy(r_hbm, r_v, dsem.at[nq])

    pl.semaphore_wait(barrier, 1 + col + n_earlier)
    slot = jnp.minimum(mine, near)
    pl.when(col == 1)(lambda: signal(x_token, at_x))
    each(earlier, lambda k: signal(token.at[slot], at_peer(k)))
    each(far_earlier, lambda k: signal(token.at[slot], at_peer(k)))

    for cp in small:
        cp.wait()

    log_c = jnp.log(cm_ref[...].astype(jnp.float32))
    ri = lax.broadcasted_iota(jnp.int32, (w, w), 0)
    ci = lax.broadcasted_iota(jnp.int32, (w, w), 1)
    log_c = jnp.sum(jnp.where(ri == ci, jnp.broadcast_to(log_c, (w, w)), 0.0), axis=1, keepdims=True)
    hi, mid, lo = split3(log_c)
    blk[...] = jnp.zeros_like(blk)
    blk[:, pl.ds(0, d)] = c_ref[...].astype(jnp.float32)
    li = lax.broadcasted_iota(jnp.int32, (w, dp), 1)
    own = blk[...]
    for at, val in ((d, hi), (d + 1, mid), (d + 2, lo)):
        own = jnp.where(li == at, val, own)
    own = jnp.where((li >= d + 3) & (li < d + 6), 1.0, own)
    cg[0, spot] = own.astype(jnp.bfloat16)

    ident = eye(LANES)

    def codes(q):
        loads[q].wait()
        for t in range(btiles):
            cells = []
            for u in range(q_w // tile):
                x = cnt_v[pl.ds(q * step + u * tile * btiles + t, tile, stride=btiles), :]
                k = q * (q_w // tile) + u
                on = jnp.broadcast_to(occ_ref[t:t + 1, k:k + 1], (tile, LANES)) != 0
                cells.append(jnp.where(on, x, -1).astype(jnp.float32).astype(jnp.bfloat16))
            code = nt(ident, jnp.concatenate(cells, axis=0)).astype(jnp.bfloat16)
            for r in range(LANES // w):
                b = t * (LANES // w) + r
                k = b // 2
                at = pl.ds((((k // hh) * 2 + b % 2) * hh + k % hh) * w, w)
                enc[0, q, at, :] = code[r * w:(r + 1) * w]

    def slopes(q):
        def one(s):
            at = pl.ds(s * sub, sub)
            slope_v[q, at, :], logc_v[q, at, :] = slope_terms(enc[0, q, at, :].astype(jnp.float32))

        repeat(nsub, one)

    def encode(q):
        codes(q)
        slopes(q)

    def x_start(q, part):
        at = pl.ds(pl.multiple_of(part * gcols, gcols), gcols)
        rcopy(enc.at[0, q, at], enc.at[1, q, at], e_s, e_r.at[q], at_x).start()

    def handed():
        return rcopy(enc.at[0, nq - 2, pl.ds(gcols, gcols)], spare, h_s, h_r, at_mate)

    def hand_on():
        rcopy(spare, enc.at[1, nq - 2, pl.ds(gcols, gcols)], e_s, e_r.at[nq - 2],
              (mate, 1 - col)).start()

    def x_starts(q):
        x_start(q, 0)
        x_start(q, 1)

    ecopies = [rcopy(enc.at[0, q], enc.at[1, q], e_s, e_r.at[q], at_x) for q in range(nq)]
    xcp = rcopy(cg.at[0, spot], cg.at[1, spot], gx_s, gx_r, at_x)

    def to_near(which, waiting):
        def one(k):
            if waiting:
                pl.semaphore_wait(token.at[k], 1)
            if k == 2:
                rcopy(cg.at[which, spot], cg.at[which, spot], g_s, w_r.at[which],
                      at_peer(k)).start()
            else:
                direct(which, k)

        each(later, one)

    def direct(which, k):
        rcopy(cg.at[which, spot], cg.at[which, spot], g_s, g_r.at[which, own_half],
              at_peer(k)).start()

    def to_earlier(which):
        each(earlier, functools.partial(direct, which))
        each(far_earlier, functools.partial(direct, which))

    def to_far(which):
        for k, cond in far_later:
            pl.when(cond & (mine > 0))(functools.partial(direct, which, k))

    def far_ready():
        @pl.when(n_far > 0)
        def _():
            pl.semaphore_wait(token.at[near], n_far)

    def relay(which):
        @pl.when(mine == 2)
        def _():
            at = cg.at[which, place_of(0, core)]
            rcopy(at, at, w_s, w_r.at[which], at_mate).wait_recv()
            for k in range(near, half):
                if which:
                    rcopy(at, at, w_s, g_r.at[which, 0], at_peer(k)).start()
                else:
                    for c in range(2):
                        rcopy(at, at, w_s, w_r.at[which], (2 * k + c, col)).start()

    to_earlier(0)
    codes(0)

    def cross():
        pl.when(col == 0)(lambda: pl.semaphore_wait(x_token, 1))
        xcp.start()
        x_starts(0)

    first = (col == 1) | (mine < near)
    pl.when(first)(cross)

    @pl.when(mine >= near)
    def _():
        far_ready()
        to_far(0)

    pl.when(jnp.logical_not(first))(cross)
    slopes(0)
    if nq > 2:
        encode(1)
    to_near(0, True)
    pl.when((mine > 0) & (mine < near))(far_ready)
    relay(0)
    pl.when(mine < near)(lambda: to_far(0))
    rload.start()
    for q in range(2, nq):
        x_start(q - 1, 0)
        if q == nq - 1:
            pl.when(core == 1)(functools.partial(x_start, q - 1, 1))
            pl.when(core == 0)(lambda: handed().start())
        else:
            x_start(q - 1, 1)
        encode(q)

    rload.wait()
    raug[pl.ds(0, d), :] = r_v[...]
    base = (d // 16) * 16
    row_term = jnp.log(rm_ref[...].astype(jnp.float32)) - lt_ref[0]
    hi, mid, lo = split3(row_term)
    tail = raug[pl.ds(base, dp - base), :].astype(jnp.float32)
    si = lax.broadcasted_iota(jnp.int32, (dp - base, rows), 0) + base
    tail = jnp.where(si < d, tail, jnp.where(si < d + 3, 1.0, 0.0))
    for at, val in ((d + 3, hi), (d + 4, mid), (d + 5, lo)):
        tail = jnp.where(si == at, val, tail)
    raug[pl.ds(base, dp - base), :] = tail.astype(jnp.bfloat16)

    def arrived(which, h, blocks):
        some = cg.at[which, pl.ds(0, blocks)]
        rcopy(some, some, g_s, g_r.at[which, h], at_mate).wait_recv()

    def to_mate(which, h, skip):
        part = cg.at[which, pl.ds((h * 2 + core) * hh + skip, hh - skip)]
        return rcopy(part, part, m_s, m_r.at[which, h], at_mate)

    def gathered(which, at):
        h = halves[at]

        def took(blocks, skip):
            arrived(which, h, blocks)
            to_mate(which, h, skip).start()

        if at and which:
            took(hh, 0)
        elif at:
            pl.when(mine < hh)(lambda: took(hh, 0))
            pl.when(mine >= hh)(lambda: took(hh - 1, 1))
        else:
            pl.when(mine == 2)(lambda: took(hh - 2, 0))
            pl.when(mine != 2)(lambda: took(hh - 1, 0))

    def from_mate_blocks(which, at):
        h = halves[at]
        if at and not which:
            pl.when(mine < hh)(lambda: to_mate(which, h, 0).wait_recv())
            pl.when(mine >= hh)(lambda: to_mate(which, h, 1).wait_recv())
        else:
            to_mate(which, h, 0).wait_recv()

    def first_chip():
        two = cg.at[0, pl.ds(0, 2)]
        rcopy(two, two, w_s, w_r.at[0], at_mate).wait_recv()
        ends = (pl.ds(0, w), pl.ds(hh * w, w))

        def both(fn):
            return jnp.concatenate([fn(at) for at in ends], axis=0)

        blocks = jnp.concatenate([cg[0, 0], cg[0, hh]], axis=0)
        for q in range(nq):
            qs = pl.ds(q * q_w, q_w)
            gap = nn(blocks, raug[:, qs])
            code = both(lambda at: enc[0, q, at, :]).astype(jnp.float32)
            slope = both(lambda at: slope_v[q, at, :])
            logc = both(lambda at: logc_v[q, at, :])
            res0[:, qs] = cell(code, slope, logc, gap).astype(jnp.bfloat16)
        s0src[...] = nt(res0[...], raug[...]).reshape(2, w, dp).astype(jnp.bfloat16)
        slot = (mine - hh) * 2 + core
        for c in range(2):
            rcopy(s0src.at[c], s0buf.at[slot], c_s, c_r, (c, col)).start()

    def block(which, first, count):
        return cg[which, pl.ds(first, count)].reshape(count * w, dp)

    def reduced(k):
        return rcopy(s2src.at[k], s2buf.at[mine], b_s, b_r, at_peer(k))

    def from_mate(h):
        return rcopy(gcol.at[pl.ds((h * 2 + 1 - core) * hh, hh)], s1buf.at[pl.ds(h * hh, hh)],
                     a_s, a_r.at[h], at_mate)

    def half_terms(h):
        for q in range(nq):
            qs = pl.ds(q * q_w, q_w)

            def cells(s):
                at = pl.ds(pl.multiple_of(h * gcols + s * subg, subg), subg)
                gap = nn(block(0, (h * gcols + s * subg) // w, subg // w), raug[:, qs])
                code = enc[0, q, at, :].astype(jnp.float32)
                got = cell(code, slope_v[q, at, :], logc_v[q, at, :], gap).astype(jnp.bfloat16)
                res[at, qs] = got
                if q == nq - 1:
                    enc[0, q, at, :] = got

            repeat(nsubg, cells)

        def terms(s):
            at = pl.ds(pl.multiple_of(h * gcols + s * subg, subg), subg)
            part = nt(res[at, :], raug[...]).reshape(subg // w, w, dp)
            gcol[pl.ds((h * gcols + s * subg) // w, subg // w)] = part

        repeat(nsubg, terms)

    def spread(h, own):
        from_mate(h).wait_recv()
        for i in range(hh):
            k = h * hh + i
            total = gcol[(h * 2 + core) * hh + i] + s1buf[k]
            s2src[k] = total.astype(s2src.dtype)
            if own:
                @pl.when(mine == k)
                def _():
                    blk[...] = total

            if i and own:
                pl.when(mine != k - 1)(lambda: reduced(k - 1).start())
            elif i == 1:
                pl.when(mine < hh)(lambda: reduced(k - 1).start())
            elif i:
                reduced(k - 1).start()

    def spread_last(h, own):
        k = h * hh + hh - 1
        if own:
            pl.when(mine != k)(lambda: reduced(k).start())
        else:
            reduced(k).start()

    ident_d = eye(dp)

    def transposed(which, h):
        def one(s):
            part = block(which, (h * gcols + s * subg) // w, subg // w)
            at = pl.ds(pl.multiple_of(h * gcols + s * subg, subg), subg)
            (cd1 if which else cd0)[:, at] = nt(ident_d, part)[:dq, :].astype(jnp.bfloat16)

        repeat(nsubg, one)

    def other_cells(q, h):
        qs = pl.ds(q * q_w, q_w)

        def cells(s):
            at = pl.ds(pl.multiple_of(h * gcols + s * subg, subg), subg)
            gap = nn(block(1, (h * gcols + s * subg) // w, subg // w), raug[:, qs])
            code = enc[1, q, at, :].astype(jnp.float32)
            slope, logc = slope_terms(code)
            enc[1, q, at, :] = cell(code, slope, logc, gap).astype(jnp.bfloat16)

        repeat(nsubg, cells)

    def other_rows(q):
        qs = pl.ds(q * q_w, q_w)
        more = nn(cd1[...], enc[1, q])[:d, :]
        rows_out[:, qs] = (rows_out[:, qs] + more) * scale_r

    xcp.wait_recv()
    to_earlier(1)
    to_near(1, False)
    gathered(0, 0)

    @pl.when(core == 1)
    def _():
        handed().wait_recv()
        hand_on()

    from_mate_blocks(0, 0)
    half_terms(own_half)
    from_mate(own_half).start()
    x_start(nq - 1, own_half)
    pl.when(mine >= hh)(first_chip)
    to_far(1)
    gathered(0, 1)
    relay(1)
    from_mate_blocks(0, 1)
    half_terms(1 - own_half)
    pl.when(mine == 0)(far_ready)
    from_mate(1 - own_half).start()
    x_start(nq - 1, 1 - own_half)
    spread(own_half, True)
    transposed(0, 0)
    spread_last(own_half, True)
    spread(1 - own_half, False)
    transposed(0, 1)
    spread_last(1 - own_half, False)
    gathered(1, 0)
    rows_out[...] = nn(cd0[...], res[...])[:d, :]

    gathered(1, 1)
    from_mate_blocks(1, 0)
    transposed(1, own_half)
    sooner = nq // 2
    for q in range(sooner):
        ecopies[q].wait_recv()
        other_cells(q, own_half)
    from_mate_blocks(1, 1)
    transposed(1, 1 - own_half)
    for q in range(sooner):
        other_cells(q, 1 - own_half)
        other_rows(q)
    for q in range(sooner, nq):
        ecopies[q].wait_recv()
        if q < nq - 1:
            other_cells(q, 0)
            other_cells(q, 1)
            other_rows(q)
        else:
            last[...] = enc[1, q]

    def summed(blocks):
        got = s2buf.at[pl.ds(0, blocks)]
        return rcopy(got, got, b_s, b_r, at_mate)

    @pl.when(mine == 0)
    def _():
        summed(hh - 1).wait_recv()
        total = blk[...]
        for k in range(1, hh):
            total = total + s2buf[k].astype(jnp.float32)
        rcopy(s0buf, s0buf, c_s, c_r, at_mate).wait_recv()
        for k in range(half):
            total = total + s0buf[k].astype(jnp.float32)
        cols_out[...] = (total * scale_c)[:, :d]

    @pl.when(mine != 0)
    def _():
        summed(half - 1).wait_recv()
        total = blk[...]
        for k in froms:
            total = total + s2buf[k].astype(jnp.float32)
        cols_out[...] = (total * scale_c)[:, :d]

    def sent(blocks):
        some = gcol.at[pl.ds(0, blocks)]
        rcopy(some, some, g_s, gx_r, at_mate).wait_send()

    pl.when(mine == 0)(lambda: sent(near - 1))
    pl.when(mine != 0)(lambda: sent(half - 1))

    @pl.when(mine == 2)
    def _():
        some = gcol.at[pl.ds(0, 3 * (half - near) // 2)]
        rcopy(some, some, w_s, gx_r, at_mate).wait_send()

    xcp.wait_send()
    def told(blocks):
        some = cg.at[0, pl.ds(0, blocks)]
        rcopy(some, some, m_s, gx_r, at_mate).wait_send()

    pl.when(mine < hh)(lambda: told(n))
    pl.when(mine >= hh)(lambda: told(n - 1))
    def crossed(pieces):
        some = cnt_v.at[pl.ds(0, pieces * gcols * q_w // (2 * LANES))]
        rcopy(some, some, e_s, gx_r, at_x).wait_send()

    @pl.when(core == 0)
    def _():
        crossed(2 * nq - 1)
        handed().wait_send()

    pl.when(core == 1)(lambda: crossed(2 * nq + 1))
    some = gcol.at[pl.ds(0, half)]
    rcopy(some, some, a_s, gx_r, at_mate).wait_send()
    pl.when(mine < hh)(lambda: summed(half - 1).wait_send())

    @pl.when(mine >= hh)
    def _():
        summed(half - 2).wait_send()
        rcopy(s0src, s0src, c_s, c_r, at_mate).wait_send()


def scratch_bytes(shapes):
    return sum(math.prod(s.shape) * jnp.dtype(s.dtype).itemsize for s in shapes)


def place(scale_r, rows_in, cols_in, cd1, last, rows_out, cols_out, end, sem):
    d, rows = rows_in.shape
    done = rows - last.shape[1]
    copies = [pltpu.make_async_copy(cols_in, cols_out, sem.at[0]),
              pltpu.make_async_copy(rows_in.at[:, pl.ds(0, done)], rows_out.at[:, pl.ds(0, done)], sem.at[1]),
              pltpu.make_async_copy(end, rows_out.at[:, pl.ds(done, rows - done)], sem.at[2])]
    copies[0].start()
    copies[1].start()
    more = nn(cd1[...], last[...])[:d, :]
    end[...] = (rows_in[:, pl.ds(done, rows - done)] + more) * scale_r
    copies[2].start()
    for cp in copies:
        cp.wait()


def body(row_embed, col_embed, counts, occupancy, row_marg, col_marg, log_total):
    n = lax.axis_size("row")
    d, rows = row_embed.shape
    w = col_embed.shape[2]
    band = counts.shape[2]
    tile = rows // occupancy.shape[0]
    q_w = 2 * tile if rows % (2 * tile) == 0 else tile
    dp = -(-(d + 6) // LANES) * LANES
    half = n // 2
    nq = rows // q_w
    dq = -(-d // 16) * 16
    btiles = band // LANES
    cfg = (n, d, dp, w, band, rows, tile, q_w,
           1.0 / math.sqrt(w * n * lax.axis_size("col")), 1.0 / math.sqrt(rows * n))
    bf, f32 = jnp.bfloat16, jnp.float32
    vm, hb, anywhere = (pl.BlockSpec(memory_space=m) for m in (pltpu.VMEM, pltpu.HBM, pl.ANY))
    dma = lambda *s: pltpu.SemaphoreType.DMA(s) if s else pltpu.SemaphoreType.DMA
    scratch = [
        pltpu.VMEM((d, rows), bf),
        pltpu.VMEM((rows * btiles, LANES), jnp.int32),
        pltpu.VMEM((dp, rows), bf),
        pltpu.VMEM((w, dp), f32),
        pltpu.VMEM((2, n, w, dp), bf),
        pltpu.VMEM((dq, band), bf),
        pltpu.VMEM((2, nq, band, q_w), bf),
        pltpu.VMEM((nq, band, q_w), f32),
        pltpu.VMEM((nq, band, q_w), f32),
        pltpu.VMEM((band, rows), bf),
        pltpu.VMEM((n, w, dp), f32),
        pltpu.VMEM((half, w, dp), f32),
        pltpu.VMEM((half, w, dp), SEND),
        pltpu.VMEM((half, w, dp), SEND),
        pltpu.VMEM((w, d), bf),
        pltpu.VMEM((occupancy.shape[2], occupancy.shape[0]), jnp.int32),
        pltpu.VMEM((1, rows), jnp.int32),
        pltpu.VMEM((1, w), jnp.int32),
        dma(nq + 5),
        dma(), dma(nq), dma(), dma(), dma(), dma(2, 2), dma(), dma(2), dma(), dma(2, 2),
        dma(), dma(2), dma(), dma(),
        pltpu.SemaphoreType.REGULAR((half // 2 + 1,)),
        pltpu.SemaphoreType.REGULAR,
        dma(), dma(), dma(), dma(),
        pltpu.VMEM((2, w, dp), bf),
        pltpu.VMEM((half, w, dp), bf),
        pltpu.VMEM((2 * w, rows), bf),
        pltpu.VMEM((band // 2, q_w), bf),
    ]
    limit = min(60 << 20, (6 << 20) + scratch_bytes(scratch[:18]) + 2 * d * rows * 4 + 28 * band * q_w)
    parts = pl.pallas_call(
        functools.partial(kernel, cfg),
        out_shape=(jax.ShapeDtypeStruct((d, rows), f32), jax.ShapeDtypeStruct((w, d), f32),
                   jax.ShapeDtypeStruct((dq, band), bf), jax.ShapeDtypeStruct((band, q_w), bf)),
        in_specs=[hb] * 6 + [pl.BlockSpec(memory_space=pltpu.SMEM)],
        out_specs=(vm,) * 4,
        scratch_shapes=scratch,
        compiler_params=pltpu.CompilerParams(
            collective_id=0, has_side_effects=True, vmem_limit_bytes=limit),
    )(
        *(pltpu.with_memory_space_constraint(x, pltpu.HBM) for x in (
            row_embed,
            jnp.transpose(col_embed, (1, 2, 0)).reshape(w, d),
            counts.reshape(rows * btiles, LANES),
            jnp.transpose(occupancy, (1, 2, 0)).reshape(occupancy.shape[2], occupancy.shape[0]),
            row_marg.reshape(1, rows),
            col_marg,
        )),
        log_total,
    )
    grad_rows, grad_cols = pl.pallas_call(
        functools.partial(place, cfg[8]),
        out_shape=(jax.ShapeDtypeStruct((d, rows), f32), jax.ShapeDtypeStruct((w, d), f32)),
        in_specs=[vm] * 4,
        out_specs=(hb, hb),
        scratch_shapes=[pltpu.VMEM((d, q_w), f32), pltpu.SemaphoreType.DMA((3,))],
        compiler_params=pltpu.CompilerParams(vmem_limit_bytes=limit),
    )(*(pltpu.with_memory_space_constraint(x, pltpu.VMEM) for x in parts))
    return grad_rows, jnp.transpose(grad_cols.reshape(1, w, d), (2, 0, 1))


def solution(mesh):
    placed = (
        P(None, "row"),
        P(None, "col", "row"),
        P("row", "col", None),
        P("row", "col", None),
        P("row"),
        P("col", "row"),
        P(),
    )
    return jax.shard_map(
        body,
        mesh=mesh,
        in_specs=placed,
        out_specs=(P(None, "row"), P(None, "col", "row")),
        check_vma=False,
    )
```

```python
import functools
import math

import jax
import jax.numpy as jnp
from jax import lax
from jax.experimental import pallas as pl
from jax.experimental.pallas import tpu as pltpu
from jax.sharding import PartitionSpec as P

LANES = 128
SEND = jnp.bfloat16


def nt(a, b):
    return lax.dot_general(a, b, (((1,), (1,)), ((), ())), preferred_element_type=jnp.float32)


def nn(a, b):
    return lax.dot_general(a, b, (((1,), (0,)), ((), ())), preferred_element_type=jnp.float32)


def split3(x):
    hi = x.astype(jnp.bfloat16).astype(jnp.float32)
    rest = x - hi
    mid = rest.astype(jnp.bfloat16).astype(jnp.float32)
    return hi, mid, rest - mid


def eye(n):
    r = lax.broadcasted_iota(jnp.int32, (n, n), 0)
    c = lax.broadcasted_iota(jnp.int32, (n, n), 1)
    return (r == c).astype(jnp.float32).astype(jnp.bfloat16)


def slope_terms(code):
    slope = jnp.where(code > 0.0, 0.1 + 0.25 * jnp.sqrt(jnp.maximum(code, 0.0)), 0.0)
    return slope, jnp.log(jnp.maximum(code, 1.0))


def cell(code, slope, logc, gap):
    return jnp.where(code == 0.0, jax.nn.sigmoid(gap), slope * (gap - logc))


def repeat(n, fn):
    if n == 1:
        fn(0)
    else:
        pl.loop(0, n)(fn)


def kernel(cfg, r_hbm, c_hbm, cnt_hbm, occ_hbm, rm_hbm, cm_hbm, lt_ref,
           rows_out, cols_out, cd1, last,
           r_v, cnt_v, raug, blk, cg, cd0, enc, slope_v, logc_v, res, gcol, s1buf, s2src, s2buf,
           c_ref, occ_ref, rm_ref, cm_ref, dsem, e_s, e_r, gx_r, g_s, g_r, w_s, w_r, m_s, m_r,
           a_s, a_r, b_s, b_r, token, x_token, c_r, h_r, s0src, s0buf, res0, spare):
    n, d, dp, w, band, rows, tile, q_w, scale_r, scale_c = cfg
    half = n // 2
    dq = -(-d // 16) * 16
    hh = half // 2
    nq = rows // q_w
    btiles = band // LANES
    sub = min(band, 256)
    nsub = band // sub
    gcols = band // 2
    subg = min(gcols, 256)
    nsubg = gcols // subg
    me = lax.axis_index("row")
    col = lax.axis_index("col")
    core = lax.rem(me, 2)
    mate = me + 1 - 2 * core
    mine = me // 2
    own_half = mine // hh
    halves = (own_half, 1 - own_half)
    froms = [lax.rem(mine - k + half, half) for k in range(1, half)]
    at_mate = (mate, col)
    at_x = (me, 1 - col)

    def place_of(k, c):
        return ((k // hh) * 2 + c) * hh + lax.rem(k, hh)

    spot = place_of(mine, core)

    def rcopy(src, dst, ss, rs, dev):
        return pltpu.make_async_remote_copy(
            src_ref=src, dst_ref=dst, send_sem=ss, recv_sem=rs,
            device_id=dev, device_id_type=pl.DeviceIdType.MESH)

    def signal(sem, dev):
        pl.semaphore_signal(sem, inc=1, device_id=dev, device_id_type=pl.DeviceIdType.MESH)

    def at_peer(k):
        return (2 * k + core, col)

    near = hh
    later = [(2, mine == 0), (1, (mine == 0) | (mine == 2))]
    later += [(k, mine < k) for k in range(3, near)]
    earlier = [(0, mine > 0), (2, (mine == 1) | (mine > 2)), (1, mine > 2)]
    earlier += [(k, mine > k) for k in range(3, near)]

    def each(pairs, fn):
        for k, cond in pairs:
            pl.when(cond)(functools.partial(fn, k))

    far_later = [(k, mine < k) for k in range(near, half)]
    far_earlier = [(k, mine > k) for k in range(near, half - 1)]
    n_earlier = jnp.where(mine == 1, 2, jnp.where(mine == 2, 1, mine))
    n_far = jnp.where(mine < near, half - near, half - 1 - mine)

    small = []
    step = q_w * btiles
    loads = [pltpu.make_async_copy(
        cnt_hbm.at[pl.ds(q * step, step), :], cnt_v.at[pl.ds(q * step, step), :], dsem.at[q])
        for q in range(nq)]
    loads[0].start()
    for k, (src, dst) in enumerate(((cm_hbm, cm_ref), (c_hbm, c_ref), (occ_hbm, occ_ref),
                                    (rm_hbm, rm_ref))):
        cp = pltpu.make_async_copy(src, dst, dsem.at[nq + k])
        cp.start()
        small.append(cp)
    for cp in loads[1:]:
        cp.start()
    barrier = pltpu.get_barrier_semaphore()
    pl.when(col == 0)(lambda: signal(barrier, at_x))
    signal(barrier, at_mate)
    each(later, lambda k: signal(barrier, at_peer(k)))
    each(far_later, lambda k: signal(barrier, at_peer(k)))

    rload = pltpu.make_async_copy(r_hbm, r_v, dsem.at[0])

    pl.semaphore_wait(barrier, 1 + col + n_earlier)
    slot = jnp.minimum(mine, near)
    pl.when(col == 1)(lambda: signal(x_token, at_x))
    each(earlier, lambda k: signal(token.at[slot - 1], at_peer(k)))
    each(far_earlier, lambda k: signal(token.at[slot - 1], at_peer(k)))

    for cp in small:
        cp.wait()

    log_c = jnp.log(cm_ref[...].astype(jnp.float32))
    ri = lax.broadcasted_iota(jnp.int32, (w, w), 0)
    ci = lax.broadcasted_iota(jnp.int32, (w, w), 1)
    log_c = jnp.sum(jnp.where(ri == ci, jnp.broadcast_to(log_c, (w, w)), 0.0), axis=1, keepdims=True)
    hi, mid, lo = split3(log_c)
    blk[...] = jnp.zeros_like(blk)
    blk[:, pl.ds(0, d)] = c_ref[...].astype(jnp.float32)
    li = lax.broadcasted_iota(jnp.int32, (w, dp), 1)
    own = blk[...]
    for at, val in ((d, hi), (d + 1, mid), (d + 2, lo)):
        own = jnp.where(li == at, val, own)
    own = jnp.where((li >= d + 3) & (li < d + 6), 1.0, own)
    cg[0, spot] = own.astype(jnp.bfloat16)

    ident = eye(LANES)

    def codes(q):
        loads[q].wait()
        for t in range(btiles):
            cells = []
            for u in range(q_w // tile):
                x = cnt_v[pl.ds(q * step + u * tile * btiles + t, tile, stride=btiles), :]
                k = q * (q_w // tile) + u
                on = jnp.broadcast_to(occ_ref[t:t + 1, k:k + 1], (tile, LANES)) != 0
                cells.append(jnp.where(on, x, -1).astype(jnp.float32).astype(jnp.bfloat16))
            code = nt(ident, jnp.concatenate(cells, axis=0)).astype(jnp.bfloat16)
            for r in range(LANES // w):
                b = t * (LANES // w) + r
                k = b // 2
                at = pl.ds((((k // hh) * 2 + b % 2) * hh + k % hh) * w, w)
                enc[0, q, at, :] = code[r * w:(r + 1) * w]

    def slopes(q):
        def one(s):
            at = pl.ds(s * sub, sub)
            slope_v[q, at, :], logc_v[q, at, :] = slope_terms(enc[0, q, at, :].astype(jnp.float32))

        repeat(nsub, one)

    def encode(q):
        codes(q)
        slopes(q)

    def x_start(q, part):
        at = pl.ds(pl.multiple_of(part * gcols, gcols), gcols)
        rcopy(enc.at[0, q, at], enc.at[1, q, at], e_s, e_r.at[q], at_x).start()

    def handed():
        return rcopy(enc.at[0, nq - 2, pl.ds(gcols, gcols)], spare, e_s, h_r, at_mate)

    def hand_on():
        rcopy(spare, enc.at[1, nq - 2, pl.ds(gcols, gcols)], e_s, e_r.at[nq - 2],
              (mate, 1 - col)).start()

    def x_starts(q):
        x_start(q, 0)
        x_start(q, 1)

    ecopies = [rcopy(enc.at[0, q], enc.at[1, q], e_s, e_r.at[q], at_x) for q in range(nq)]
    xcp = rcopy(cg.at[0, spot], cg.at[1, spot], g_s, gx_r, at_x)

    def to_near(which, waiting):
        def one(k):
            if waiting:
                pl.semaphore_wait(token.at[k - 1], 1)
            if k == 2:
                rcopy(cg.at[which, spot], cg.at[which, spot], g_s, w_r.at[which],
                      at_peer(k)).start()
            else:
                direct(which, k)

        each(later, one)

    def direct(which, k):
        rcopy(cg.at[which, spot], cg.at[which, spot], g_s, g_r.at[which, own_half],
              at_peer(k)).start()

    def to_earlier(which):
        each(earlier, functools.partial(direct, which))
        each(far_earlier, functools.partial(direct, which))

    def to_far(which):
        for k, cond in far_later:
            pl.when(cond & (mine > 0))(functools.partial(direct, which, k))

    def far_ready():
        @pl.when(n_far > 0)
        def _():
            pl.semaphore_wait(token.at[near - 1], n_far)

    def relay(which):
        @pl.when(mine == 2)
        def _():
            at = cg.at[which, place_of(0, core)]
            rcopy(at, at, w_s, w_r.at[which], at_mate).wait_recv()
            for k in range(near, half):
                if which:
                    rcopy(at, at, w_s, g_r.at[which, 0], at_peer(k)).start()
                else:
                    for c in range(2):
                        rcopy(at, at, w_s, w_r.at[which], (2 * k + c, col)).start()

    to_earlier(0)
    codes(0)

    def cross():
        pl.when(col == 0)(lambda: pl.semaphore_wait(x_token, 1))
        xcp.start()
        x_starts(0)

    first = (col == 1) | (mine < near)
    pl.when(first)(cross)

    @pl.when(mine >= near)
    def _():
        far_ready()
        to_far(0)

    pl.when(jnp.logical_not(first))(cross)
    slopes(0)
    if nq > 2:
        encode(1)
    to_near(0, True)
    pl.when((mine > 0) & (mine < near))(far_ready)
    relay(0)
    pl.when(mine < near)(lambda: to_far(0))
    rload.start()
    for q in range(2, nq):
        x_start(q - 1, 0)
        if q == nq - 1:
            pl.when(core == 1)(functools.partial(x_start, q - 1, 1))
            pl.when(core == 0)(lambda: handed().start())
        else:
            x_start(q - 1, 1)
        encode(q)

    rload.wait()
    raug[pl.ds(0, d), :] = r_v[...]
    base = (d // 16) * 16
    row_term = jnp.log(rm_ref[...].astype(jnp.float32)) - lt_ref[0]
    hi, mid, lo = split3(row_term)
    tail = raug[pl.ds(base, dp - base), :].astype(jnp.float32)
    si = lax.broadcasted_iota(jnp.int32, (dp - base, rows), 0) + base
    tail = jnp.where(si < d, tail, jnp.where(si < d + 3, 1.0, 0.0))
    for at, val in ((d + 3, hi), (d + 4, mid), (d + 5, lo)):
        tail = jnp.where(si == at, val, tail)
    raug[pl.ds(base, dp - base), :] = tail.astype(jnp.bfloat16)

    def arrived(which, h, blocks):
        some = cg.at[which, pl.ds(0, blocks)]
        rcopy(some, some, g_s, g_r.at[which, h], at_mate).wait_recv()

    def to_mate(which, h, skip):
        part = cg.at[which, pl.ds((h * 2 + core) * hh + skip, hh - skip)]
        return rcopy(part, part, m_s, m_r.at[which, h], at_mate)

    def gathered(which, at):
        h = halves[at]

        def took(blocks, skip):
            arrived(which, h, blocks)
            to_mate(which, h, skip).start()

        if at and which:
            took(hh, 0)
        elif at:
            pl.when(mine < hh)(lambda: took(hh, 0))
            pl.when(mine >= hh)(lambda: took(hh - 1, 1))
        else:
            pl.when(mine == 2)(lambda: took(hh - 2, 0))
            pl.when(mine != 2)(lambda: took(hh - 1, 0))

    def from_mate_blocks(which, at):
        h = halves[at]
        if at and not which:
            pl.when(mine < hh)(lambda: to_mate(which, h, 0).wait_recv())
            pl.when(mine >= hh)(lambda: to_mate(which, h, 1).wait_recv())
        else:
            to_mate(which, h, 0).wait_recv()

    def first_chip():
        two = cg.at[0, pl.ds(0, 2)]
        rcopy(two, two, w_s, w_r.at[0], at_mate).wait_recv()
        ends = (pl.ds(0, w), pl.ds(hh * w, w))

        def both(fn):
            return jnp.concatenate([fn(at) for at in ends], axis=0)

        blocks = jnp.concatenate([cg[0, 0], cg[0, hh]], axis=0)
        for q in range(nq):
            qs = pl.ds(q * q_w, q_w)
            gap = nn(blocks, raug[:, qs])
            code = both(lambda at: enc[0, q, at, :]).astype(jnp.float32)
            slope = both(lambda at: slope_v[q, at, :])
            logc = both(lambda at: logc_v[q, at, :])
            res0[:, qs] = cell(code, slope, logc, gap).astype(jnp.bfloat16)
        s0src[...] = nt(res0[...], raug[...]).reshape(2, w, dp).astype(jnp.bfloat16)
        slot = (mine - hh) * 2 + core
        for c in range(2):
            rcopy(s0src.at[c], s0buf.at[slot], b_s, c_r, (c, col)).start()

    def block(which, first, count):
        return cg[which, pl.ds(first, count)].reshape(count * w, dp)

    def reduced(k):
        return rcopy(s2src.at[k], s2buf.at[mine], b_s, b_r, at_peer(k))

    def from_mate(h):
        return rcopy(gcol.at[pl.ds((h * 2 + 1 - core) * hh, hh)], s1buf.at[pl.ds(h * hh, hh)],
                     a_s, a_r.at[h], at_mate)

    def half_terms(h):
        for q in range(nq):
            qs = pl.ds(q * q_w, q_w)

            def cells(s):
                at = pl.ds(pl.multiple_of(h * gcols + s * subg, subg), subg)
                gap = nn(block(0, (h * gcols + s * subg) // w, subg // w), raug[:, qs])
                code = enc[0, q, at, :].astype(jnp.float32)
                got = cell(code, slope_v[q, at, :], logc_v[q, at, :], gap).astype(jnp.bfloat16)
                res[at, qs] = got
                if q == nq - 1:
                    enc[0, q, at, :] = got

            repeat(nsubg, cells)

        def terms(s):
            at = pl.ds(pl.multiple_of(h * gcols + s * subg, subg), subg)
            part = nt(res[at, :], raug[...]).reshape(subg // w, w, dp)
            gcol[pl.ds((h * gcols + s * subg) // w, subg // w)] = part

        repeat(nsubg, terms)

    def spread(h, own):
        from_mate(h).wait_recv()
        for i in range(hh):
            k = h * hh + i
            total = gcol[(h * 2 + core) * hh + i] + s1buf[k]
            s2src[k] = total.astype(s2src.dtype)
            if own:
                @pl.when(mine == k)
                def _():
                    blk[...] = total

            if i and own:
                pl.when(mine != k - 1)(lambda: reduced(k - 1).start())
            elif i == 1:
                pl.when(mine < hh)(lambda: reduced(k - 1).start())
            elif i:
                reduced(k - 1).start()

    def spread_last(h, own):
        k = h * hh + hh - 1
        if own:
            pl.when(mine != k)(lambda: reduced(k).start())
        else:
            reduced(k).start()

    ident_d = eye(dp)

    def transposed(which, h):
        def one(s):
            part = block(which, (h * gcols + s * subg) // w, subg // w)
            at = pl.ds(pl.multiple_of(h * gcols + s * subg, subg), subg)
            (cd1 if which else cd0)[:, at] = nt(ident_d, part)[:dq, :].astype(jnp.bfloat16)

        repeat(nsubg, one)

    def other_cells(q, h):
        qs = pl.ds(q * q_w, q_w)

        def cells(s):
            at = pl.ds(pl.multiple_of(h * gcols + s * subg, subg), subg)
            gap = nn(block(1, (h * gcols + s * subg) // w, subg // w), raug[:, qs])
            code = enc[1, q, at, :].astype(jnp.float32)
            slope, logc = slope_terms(code)
            enc[1, q, at, :] = cell(code, slope, logc, gap).astype(jnp.bfloat16)

        repeat(nsubg, cells)

    def other_rows(q):
        qs = pl.ds(q * q_w, q_w)
        more = nn(cd1[...], enc[1, q])[:d, :]
        rows_out[:, qs] = (rows_out[:, qs] + more) * scale_r

    xcp.wait_recv()
    to_earlier(1)
    to_near(1, False)
    gathered(0, 0)

    @pl.when(core == 1)
    def _():
        handed().wait_recv()
        hand_on()

    from_mate_blocks(0, 0)
    half_terms(own_half)
    from_mate(own_half).start()
    x_start(nq - 1, own_half)
    pl.when(mine >= hh)(first_chip)
    to_far(1)
    gathered(0, 1)
    relay(1)
    from_mate_blocks(0, 1)
    half_terms(1 - own_half)
    pl.when(mine == 0)(far_ready)
    from_mate(1 - own_half).start()
    x_start(nq - 1, 1 - own_half)
    spread(own_half, True)
    transposed(0, 0)
    spread_last(own_half, True)
    spread(1 - own_half, False)
    transposed(0, 1)
    spread_last(1 - own_half, False)
    gathered(1, 0)
    rows_out[...] = nn(cd0[...], res[...])[:d, :]

    gathered(1, 1)
    from_mate_blocks(1, 0)
    transposed(1, own_half)
    sooner = nq // 2
    for q in range(sooner):
        ecopies[q].wait_recv()
        other_cells(q, own_half)
    from_mate_blocks(1, 1)
    transposed(1, 1 - own_half)
    for q in range(sooner):
        other_cells(q, 1 - own_half)
        other_rows(q)
    for q in range(sooner, nq):
        ecopies[q].wait_recv()
        if q < nq - 1:
            other_cells(q, 0)
            other_cells(q, 1)
            other_rows(q)
        else:
            last[...] = enc[1, q]

    def summed(blocks):
        got = s2buf.at[pl.ds(0, blocks)]
        return rcopy(got, got, b_s, b_r, at_mate)

    @pl.when(mine == 0)
    def _():
        summed(hh - 1).wait_recv()
        total = blk[...]
        for k in range(1, hh):
            total = total + s2buf[k].astype(jnp.float32)
        rcopy(s0buf, s0buf, b_s, c_r, at_mate).wait_recv()
        for k in range(half):
            total = total + s0buf[k].astype(jnp.float32)
        cols_out[...] = (total * scale_c)[:, :d]

    @pl.when(mine != 0)
    def _():
        summed(half - 1).wait_recv()
        total = blk[...]
        for k in froms:
            total = total + s2buf[k].astype(jnp.float32)
        cols_out[...] = (total * scale_c)[:, :d]

    def sent(blocks):
        some = cg.at[0, pl.ds(0, blocks)]
        rcopy(some, some, g_s, gx_r, at_mate).wait_send()

    pl.when(mine == 0)(lambda: sent(2 * near - 1))
    pl.when(mine != 0)(lambda: sent(n - 1))

    @pl.when(mine == 2)
    def _():
        some = gcol.at[pl.ds(0, 3 * (half - near) // 2)]
        rcopy(some, some, w_s, gx_r, at_mate).wait_send()

    def told(blocks):
        some = cg.at[0, pl.ds(0, blocks)]
        rcopy(some, some, m_s, gx_r, at_mate).wait_send()

    pl.when(mine < hh)(lambda: told(n))
    pl.when(mine >= hh)(lambda: told(n - 1))
    def crossed(pieces):
        some = cnt_v.at[pl.ds(0, pieces * gcols * q_w // (2 * LANES))]
        rcopy(some, some, e_s, gx_r, at_x).wait_send()

    pl.when(core == 0)(lambda: crossed(2 * nq))
    pl.when(core == 1)(lambda: crossed(2 * nq + 1))
    some = gcol.at[pl.ds(0, half)]
    rcopy(some, some, a_s, gx_r, at_mate).wait_send()
    pl.when(mine < hh)(lambda: summed(half - 1).wait_send())
    pl.when(mine >= hh)(lambda: summed(half).wait_send())


def scratch_bytes(shapes):
    return sum(math.prod(s.shape) * jnp.dtype(s.dtype).itemsize for s in shapes)


def place(scale_r, rows_in, cols_in, cd1, last, rows_out, cols_out, end, sem):
    d, rows = rows_in.shape
    done = rows - last.shape[1]
    copies = [pltpu.make_async_copy(cols_in, cols_out, sem.at[0]),
              pltpu.make_async_copy(rows_in.at[:, pl.ds(0, done)], rows_out.at[:, pl.ds(0, done)], sem.at[1]),
              pltpu.make_async_copy(end, rows_out.at[:, pl.ds(done, rows - done)], sem.at[2])]
    copies[0].start()
    copies[1].start()
    more = nn(cd1[...], last[...])[:d, :]
    end[...] = (rows_in[:, pl.ds(done, rows - done)] + more) * scale_r
    copies[2].start()
    for cp in copies:
        cp.wait()


def body(row_embed, col_embed, counts, occupancy, row_marg, col_marg, log_total):
    n = lax.axis_size("row")
    d, rows = row_embed.shape
    w = col_embed.shape[2]
    band = counts.shape[2]
    tile = rows // occupancy.shape[0]
    q_w = 2 * tile if rows % (2 * tile) == 0 else tile
    dp = -(-(d + 6) // LANES) * LANES
    half = n // 2
    nq = rows // q_w
    dq = -(-d // 16) * 16
    btiles = band // LANES
    cfg = (n, d, dp, w, band, rows, tile, q_w,
           1.0 / math.sqrt(w * n * lax.axis_size("col")), 1.0 / math.sqrt(rows * n))
    bf, f32 = jnp.bfloat16, jnp.float32
    vm, hb, anywhere = (pl.BlockSpec(memory_space=m) for m in (pltpu.VMEM, pltpu.HBM, pl.ANY))
    dma = lambda *s: pltpu.SemaphoreType.DMA(s) if s else pltpu.SemaphoreType.DMA
    scratch = [
        pltpu.VMEM((d, rows), bf),
        pltpu.VMEM((rows * btiles, LANES), jnp.int32),
        pltpu.VMEM((dp, rows), bf),
        pltpu.VMEM((w, dp), f32),
        pltpu.VMEM((2, n, w, dp), bf),
        pltpu.VMEM((dq, band), bf),
        pltpu.VMEM((2, nq, band, q_w), bf),
        pltpu.VMEM((nq, band, q_w), f32),
        pltpu.VMEM((nq, band, q_w), f32),
        pltpu.VMEM((band, rows), bf),
        pltpu.VMEM((n, w, dp), f32),
        pltpu.VMEM((half, w, dp), f32),
        pltpu.VMEM((half, w, dp), SEND),
        pltpu.VMEM((half, w, dp), SEND),
        pltpu.VMEM((w, d), bf),
        pltpu.VMEM((occupancy.shape[2], occupancy.shape[0]), jnp.int32),
        pltpu.VMEM((1, rows), jnp.int32),
        pltpu.VMEM((1, w), jnp.int32),
        dma(nq + 4),
        dma(), dma(nq), dma(), dma(), dma(2, 2), dma(), dma(2), dma(), dma(2, 2),
        dma(), dma(2), dma(), dma(),
        pltpu.SemaphoreType.REGULAR((half // 2,)),
        pltpu.SemaphoreType.REGULAR,
        dma(), dma(),
        pltpu.VMEM((2, w, dp), bf),
        pltpu.VMEM((half, w, dp), bf),
        pltpu.VMEM((2 * w, rows), bf),
        pltpu.VMEM((band // 2, q_w), bf),
    ]
    limit = min(60 << 20, (6 << 20) + scratch_bytes(scratch[:18]) + 2 * d * rows * 4 + 28 * band * q_w)
    parts = pl.pallas_call(
        functools.partial(kernel, cfg),
        out_shape=(jax.ShapeDtypeStruct((d, rows), f32), jax.ShapeDtypeStruct((w, d), f32),
                   jax.ShapeDtypeStruct((dq, band), bf), jax.ShapeDtypeStruct((band, q_w), bf)),
        in_specs=[hb] * 6 + [pl.BlockSpec(memory_space=pltpu.SMEM)],
        out_specs=(vm,) * 4,
        scratch_shapes=scratch,
        compiler_params=pltpu.CompilerParams(
            collective_id=0, has_side_effects=True, vmem_limit_bytes=limit),
    )(
        *(pltpu.with_memory_space_constraint(x, pltpu.HBM) for x in (
            row_embed,
            jnp.transpose(col_embed, (1, 2, 0)).reshape(w, d),
            counts.reshape(rows * btiles, LANES),
            jnp.transpose(occupancy, (1, 2, 0)).reshape(occupancy.shape[2], occupancy.shape[0]),
            row_marg.reshape(1, rows),
            col_marg,
        )),
        log_total,
    )
    grad_rows, grad_cols = pl.pallas_call(
        functools.partial(place, cfg[8]),
        out_shape=(jax.ShapeDtypeStruct((d, rows), f32), jax.ShapeDtypeStruct((w, d), f32)),
        in_specs=[vm] * 4,
        out_specs=(hb, hb),
        scratch_shapes=[pltpu.VMEM((d, q_w), f32), pltpu.SemaphoreType.DMA((3,))],
        compiler_params=pltpu.CompilerParams(vmem_limit_bytes=limit),
    )(*(pltpu.with_memory_space_constraint(x, pltpu.VMEM) for x in parts))
    return grad_rows, jnp.transpose(grad_cols.reshape(1, w, d), (2, 0, 1))


def solution(mesh):
    placed = (
        P(None, "row"),
        P(None, "col", "row"),
        P("row", "col", None),
        P("row", "col", None),
        P("row"),
        P("col", "row"),
        P(),
    )
    return jax.shard_map(
        body,
        mesh=mesh,
        in_specs=placed,
        out_specs=(P(None, "row"), P(None, "col", "row")),
        check_vma=False,
    )
```

```python
import functools
import math

import jax
import jax.numpy as jnp
from jax import lax
from jax.experimental import pallas as pl
from jax.experimental.pallas import tpu as pltpu
from jax.sharding import PartitionSpec as P

LANES = 128
SEND = jnp.bfloat16


def nt(a, b):
    return lax.dot_general(a, b, (((1,), (1,)), ((), ())), preferred_element_type=jnp.float32)


def nn(a, b):
    return lax.dot_general(a, b, (((1,), (0,)), ((), ())), preferred_element_type=jnp.float32)


def split3(x):
    hi = x.astype(jnp.bfloat16).astype(jnp.float32)
    rest = x - hi
    mid = rest.astype(jnp.bfloat16).astype(jnp.float32)
    return hi, mid, rest - mid


def eye(n):
    r = lax.broadcasted_iota(jnp.int32, (n, n), 0)
    c = lax.broadcasted_iota(jnp.int32, (n, n), 1)
    return (r == c).astype(jnp.float32).astype(jnp.bfloat16)


def slope_terms(code):
    slope = jnp.where(code > 0.0, 0.1 + 0.25 * jnp.sqrt(jnp.maximum(code, 0.0)), 0.0)
    return slope, jnp.log(jnp.maximum(code, 1.0))


def cell(code, slope, logc, gap):
    return jnp.where(code == 0.0, jax.nn.sigmoid(gap), slope * (gap - logc))


def repeat(n, fn):
    if n == 1:
        fn(0)
    else:
        pl.loop(0, n)(fn)


def kernel(cfg, r_hbm, c_hbm, cnt_hbm, occ_hbm, rm_hbm, cm_hbm, lt_ref,
           rows_out, cols_out, cd1, last,
           r_v, cnt_v, raug, blk, cg, cd0, enc, slope_v, logc_v, res, gcol, s1buf, s2src, s2buf,
           c_ref, occ_ref, rm_ref, cm_ref, dsem, e_s, e_r, gx_r, g_s, g_r, w_s, w_r, m_s, m_r,
           a_s, a_r, b_s, b_r, token, x_token, c_r, h_r, s0src, s0buf, res0, spare):
    n, d, dp, w, band, rows, tile, q_w, scale_r, scale_c = cfg
    half = n // 2
    dq = -(-d // 16) * 16
    hh = half // 2
    nq = rows // q_w
    btiles = band // LANES
    sub = min(band, 256)
    nsub = band // sub
    gcols = band // 2
    subg = min(gcols, 256)
    nsubg = gcols // subg
    me = lax.axis_index("row")
    col = lax.axis_index("col")
    core = lax.rem(me, 2)
    mate = me + 1 - 2 * core
    mine = me // 2
    own_half = mine // hh
    halves = (own_half, 1 - own_half)
    froms = [lax.rem(mine - k + half, half) for k in range(1, half)]
    at_mate = (mate, col)
    at_x = (me, 1 - col)

    def place_of(k, c):
        return ((k // hh) * 2 + c) * hh + lax.rem(k, hh)

    spot = place_of(mine, core)

    def rcopy(src, dst, ss, rs, dev):
        return pltpu.make_async_remote_copy(
            src_ref=src, dst_ref=dst, send_sem=ss, recv_sem=rs,
            device_id=dev, device_id_type=pl.DeviceIdType.MESH)

    def signal(sem, dev):
        pl.semaphore_signal(sem, inc=1, device_id=dev, device_id_type=pl.DeviceIdType.MESH)

    def at_peer(k):
        return (2 * k + core, col)

    near = hh
    later = [(2, mine == 0), (1, (mine == 0) | (mine == 2))]
    later += [(k, mine < k) for k in range(3, near)]
    earlier = [(0, mine > 0), (2, (mine == 1) | (mine > 2)), (1, mine > 2)]
    earlier += [(k, mine > k) for k in range(3, near)]

    def each(pairs, fn):
        for k, cond in pairs:
            pl.when(cond)(functools.partial(fn, k))

    far_later = [(k, mine < k) for k in range(near, half)]
    far_earlier = [(k, mine > k) for k in range(near, half - 1)]
    n_earlier = jnp.where(mine == 1, 2, jnp.where(mine == 2, 1, mine))
    n_far = jnp.where(mine < near, half - near, half - 1 - mine)

    small = []
    step = q_w * btiles
    loads = [pltpu.make_async_copy(
        cnt_hbm.at[pl.ds(q * step, step), :], cnt_v.at[pl.ds(q * step, step), :], dsem.at[q])
        for q in range(nq)]
    loads[0].start()
    for k, (src, dst) in enumerate(((cm_hbm, cm_ref), (c_hbm, c_ref), (occ_hbm, occ_ref),
                                    (rm_hbm, rm_ref))):
        cp = pltpu.make_async_copy(src, dst, dsem.at[nq + k])
        cp.start()
        small.append(cp)
    for cp in loads[1:]:
        cp.start()
    barrier = pltpu.get_barrier_semaphore()
    pl.when(col == 0)(lambda: signal(barrier, at_x))
    signal(barrier, at_mate)
    each(later, lambda k: signal(barrier, at_peer(k)))
    each(far_later, lambda k: signal(barrier, at_peer(k)))

    rload = pltpu.make_async_copy(r_hbm, r_v, dsem.at[0])

    pl.semaphore_wait(barrier, 1 + col + n_earlier)
    slot = jnp.minimum(mine, near)
    pl.when(col == 1)(lambda: signal(x_token, at_x))
    each(earlier, lambda k: signal(token.at[slot - 1], at_peer(k)))
    each(far_earlier, lambda k: signal(token.at[slot - 1], at_peer(k)))

    for cp in small:
        cp.wait()

    log_c = jnp.log(cm_ref[...].astype(jnp.float32))
    ri = lax.broadcasted_iota(jnp.int32, (w, w), 0)
    ci = lax.broadcasted_iota(jnp.int32, (w, w), 1)
    log_c = jnp.sum(jnp.where(ri == ci, jnp.broadcast_to(log_c, (w, w)), 0.0), axis=1, keepdims=True)
    hi, mid, lo = split3(log_c)
    blk[...] = jnp.zeros_like(blk)
    blk[:, pl.ds(0, d)] = c_ref[...].astype(jnp.float32)
    li = lax.broadcasted_iota(jnp.int32, (w, dp), 1)
    own = blk[...]
    for at, val in ((d, hi), (d + 1, mid), (d + 2, lo)):
        own = jnp.where(li == at, val, own)
    own = jnp.where((li >= d + 3) & (li < d + 6), 1.0, own)
    cg[0, spot] = own.astype(jnp.bfloat16)

    ident = eye(LANES)

    def codes(q):
        loads[q].wait()
        for t in range(btiles):
            cells = []
            for u in range(q_w // tile):
                x = cnt_v[pl.ds(q * step + u * tile * btiles + t, tile, stride=btiles), :]
                k = q * (q_w // tile) + u
                on = jnp.broadcast_to(occ_ref[t:t + 1, k:k + 1], (tile, LANES)) != 0
                cells.append(jnp.where(on, x, -1).astype(jnp.float32).astype(jnp.bfloat16))
            code = nt(ident, jnp.concatenate(cells, axis=0)).astype(jnp.bfloat16)
            for r in range(LANES // w):
                b = t * (LANES // w) + r
                k = b // 2
                at = pl.ds((((k // hh) * 2 + b % 2) * hh + k % hh) * w, w)
                enc[0, q, at, :] = code[r * w:(r + 1) * w]

    def slopes(q):
        def one(s):
            at = pl.ds(s * sub, sub)
            slope_v[q, at, :], logc_v[q, at, :] = slope_terms(enc[0, q, at, :].astype(jnp.float32))

        repeat(nsub, one)

    def encode(q):
        codes(q)
        slopes(q)

    def x_start(q, part):
        at = pl.ds(pl.multiple_of(part * gcols, gcols), gcols)
        rcopy(enc.at[0, q, at], enc.at[1, q, at], e_s, e_r.at[q], at_x).start()

    def handed():
        return rcopy(enc.at[0, nq - 2, pl.ds(gcols, gcols)], spare, e_s, h_r, at_mate)

    def hand_on():
        rcopy(spare, enc.at[1, nq - 2, pl.ds(gcols, gcols)], e_s, e_r.at[nq - 2],
              (mate, 1 - col)).start()

    def x_starts(q):
        x_start(q, 0)
        x_start(q, 1)

    ecopies = [rcopy(enc.at[0, q], enc.at[1, q], e_s, e_r.at[q], at_x) for q in range(nq)]
    xcp = rcopy(cg.at[0, spot], cg.at[1, spot], g_s, gx_r, at_x)

    def to_near(which, waiting):
        def one(k):
            if waiting:
                pl.semaphore_wait(token.at[k - 1], 1)
            if k == 2:
                rcopy(cg.at[which, spot], cg.at[which, spot], g_s, w_r.at[which],
                      at_peer(k)).start()
            else:
                direct(which, k)

        each(later, one)

    def direct(which, k):
        rcopy(cg.at[which, spot], cg.at[which, spot], g_s, g_r.at[which, own_half],
              at_peer(k)).start()

    def to_earlier(which):
        each(earlier, functools.partial(direct, which))
        each(far_earlier, functools.partial(direct, which))

    def to_far(which):
        for k, cond in far_later:
            pl.when(cond & (mine > 0))(functools.partial(direct, which, k))

    def far_ready():
        @pl.when(n_far > 0)
        def _():
            pl.semaphore_wait(token.at[near - 1], n_far)

    def relay(which):
        @pl.when(mine == 2)
        def _():
            at = cg.at[which, place_of(0, core)]
            rcopy(at, at, w_s, w_r.at[which], at_mate).wait_recv()
            for k in range(near, half):
                if which:
                    rcopy(at, at, w_s, g_r.at[which, 0], at_peer(k)).start()
                else:
                    for c in range(2):
                        rcopy(at, at, w_s, w_r.at[which], (2 * k + c, col)).start()

    to_earlier(0)
    codes(0)

    def cross():
        pl.when(col == 0)(lambda: pl.semaphore_wait(x_token, 1))
        xcp.start()
        x_starts(0)

    first = (col == 1) | (mine < near)
    pl.when(first)(cross)

    @pl.when(mine >= near)
    def _():
        far_ready()
        to_far(0)

    pl.when(jnp.logical_not(first))(cross)
    slopes(0)
    if nq > 2:
        encode(1)
    to_near(0, True)
    pl.when((mine > 0) & (mine < near))(far_ready)
    relay(0)
    pl.when(mine < near)(lambda: to_far(0))
    rload.start()
    for q in range(2, nq):
        x_start(q - 1, 0)
        if q == nq - 1:
            pl.when(core == 1)(functools.partial(x_start, q - 1, 1))
            pl.when(core == 0)(lambda: handed().start())
        else:
            x_start(q - 1, 1)
        encode(q)

    rload.wait()
    raug[pl.ds(0, d), :] = r_v[...]
    base = (d // 16) * 16
    row_term = jnp.log(rm_ref[...].astype(jnp.float32)) - lt_ref[0]
    hi, mid, lo = split3(row_term)
    tail = raug[pl.ds(base, dp - base), :].astype(jnp.float32)
    si = lax.broadcasted_iota(jnp.int32, (dp - base, rows), 0) + base
    tail = jnp.where(si < d, tail, jnp.where(si < d + 3, 1.0, 0.0))
    for at, val in ((d + 3, hi), (d + 4, mid), (d + 5, lo)):
        tail = jnp.where(si == at, val, tail)
    raug[pl.ds(base, dp - base), :] = tail.astype(jnp.bfloat16)

    def arrived(which, h, blocks):
        some = cg.at[which, pl.ds(0, blocks)]
        rcopy(some, some, g_s, g_r.at[which, h], at_mate).wait_recv()

    def to_mate(which, h, skip):
        part = cg.at[which, pl.ds((h * 2 + core) * hh + skip, hh - skip)]
        return rcopy(part, part, m_s, m_r.at[which, h], at_mate)

    def gathered(which, at):
        h = halves[at]

        def took(blocks, skip):
            arrived(which, h, blocks)
            to_mate(which, h, skip).start()

        if at and which:
            took(hh, 0)
        elif at:
            pl.when(mine < hh)(lambda: took(hh, 0))
            pl.when(mine >= hh)(lambda: took(hh - 1, 1))
        else:
            pl.when(mine == 2)(lambda: took(hh - 2, 0))
            pl.when(mine != 2)(lambda: took(hh - 1, 0))

    def from_mate_blocks(which, at):
        h = halves[at]
        if at and not which:
            pl.when(mine < hh)(lambda: to_mate(which, h, 0).wait_recv())
            pl.when(mine >= hh)(lambda: to_mate(which, h, 1).wait_recv())
        else:
            to_mate(which, h, 0).wait_recv()

    def first_chip():
        two = cg.at[0, pl.ds(0, 2)]
        rcopy(two, two, w_s, w_r.at[0], at_mate).wait_recv()
        ends = (pl.ds(0, w), pl.ds(hh * w, w))

        def both(fn):
            return jnp.concatenate([fn(at) for at in ends], axis=0)

        blocks = jnp.concatenate([cg[0, 0], cg[0, hh]], axis=0)
        for q in range(nq):
            qs = pl.ds(q * q_w, q_w)
            gap = nn(blocks, raug[:, qs])
            code = both(lambda at: enc[0, q, at, :]).astype(jnp.float32)
            slope = both(lambda at: slope_v[q, at, :])
            logc = both(lambda at: logc_v[q, at, :])
            res0[:, qs] = cell(code, slope, logc, gap).astype(jnp.bfloat16)
        s0src[...] = nt(res0[...], raug[...]).reshape(2, w, dp).astype(jnp.bfloat16)
        slot = (mine - hh) * 2 + core
        for c in range(2):
            rcopy(s0src.at[c], s0buf.at[slot], b_s, c_r, (c, col)).start()

    def block(which, first, count):
        return cg[which, pl.ds(first, count)].reshape(count * w, dp)

    def reduced(k):
        return rcopy(s2src.at[k], s2buf.at[mine], b_s, b_r, at_peer(k))

    def from_mate(h):
        return rcopy(gcol.at[pl.ds((h * 2 + 1 - core) * hh, hh)], s1buf.at[pl.ds(h * hh, hh)],
                     a_s, a_r.at[h], at_mate)

    def half_terms(h):
        for q in range(nq):
            qs = pl.ds(q * q_w, q_w)

            def cells(s):
                at = pl.ds(pl.multiple_of(h * gcols + s * subg, subg), subg)
                gap = nn(block(0, (h * gcols + s * subg) // w, subg // w), raug[:, qs])
                code = enc[0, q, at, :].astype(jnp.float32)
                got = cell(code, slope_v[q, at, :], logc_v[q, at, :], gap).astype(jnp.bfloat16)
                res[at, qs] = got
                if q == nq - 1:
                    enc[0, q, at, :] = got

            repeat(nsubg, cells)

        def terms(s):
            at = pl.ds(pl.multiple_of(h * gcols + s * subg, subg), subg)
            part = nt(res[at, :], raug[...]).reshape(subg // w, w, dp)
            gcol[pl.ds((h * gcols + s * subg) // w, subg // w)] = part

        repeat(nsubg, terms)

    turns = [0, 2, 1] + list(range(3, hh))

    def spread(h, own):
        from_mate(h).wait_recv()
        held = None
        for i in turns:
            k = h * hh + i
            total = gcol[(h * 2 + core) * hh + i] + s1buf[k]
            s2src[k] = total.astype(s2src.dtype)
            if own:
                @pl.when(mine == k)
                def _():
                    blk[...] = total

            if held is not None:
                send_terms(h, held, own)
            held = i

    def send_terms(h, i, own):
        k = h * hh + i
        if own:
            pl.when(mine != k)(lambda: reduced(k).start())
        elif i:
            reduced(k).start()
        else:
            pl.when(mine < hh)(lambda: reduced(k).start())

    def spread_last(h, own):
        send_terms(h, turns[-1], own)

    ident_d = eye(dp)

    def transposed(which, h):
        def one(s):
            part = block(which, (h * gcols + s * subg) // w, subg // w)
            at = pl.ds(pl.multiple_of(h * gcols + s * subg, subg), subg)
            (cd1 if which else cd0)[:, at] = nt(ident_d, part)[:dq, :].astype(jnp.bfloat16)

        repeat(nsubg, one)

    def other_cells(q, h):
        qs = pl.ds(q * q_w, q_w)

        def cells(s):
            at = pl.ds(pl.multiple_of(h * gcols + s * subg, subg), subg)
            gap = nn(block(1, (h * gcols + s * subg) // w, subg // w), raug[:, qs])
            code = enc[1, q, at, :].astype(jnp.float32)
            slope, logc = slope_terms(code)
            enc[1, q, at, :] = cell(code, slope, logc, gap).astype(jnp.bfloat16)

        repeat(nsubg, cells)

    def other_rows(q):
        qs = pl.ds(q * q_w, q_w)
        more = nn(cd1[...], enc[1, q])[:d, :]
        rows_out[:, qs] = (rows_out[:, qs] + more) * scale_r

    xcp.wait_recv()
    to_earlier(1)
    to_near(1, False)
    gathered(0, 0)

    @pl.when(core == 1)
    def _():
        handed().wait_recv()
        hand_on()

    from_mate_blocks(0, 0)
    half_terms(own_half)
    from_mate(own_half).start()
    x_start(nq - 1, own_half)
    pl.when(mine >= hh)(first_chip)
    to_far(1)
    gathered(0, 1)
    relay(1)
    from_mate_blocks(0, 1)
    half_terms(1 - own_half)
    pl.when(mine == 0)(far_ready)
    from_mate(1 - own_half).start()
    x_start(nq - 1, 1 - own_half)
    spread(own_half, True)
    transposed(0, 0)
    spread_last(own_half, True)
    spread(1 - own_half, False)
    transposed(0, 1)
    spread_last(1 - own_half, False)
    gathered(1, 0)
    rows_out[...] = nn(cd0[...], res[...])[:d, :]

    gathered(1, 1)
    from_mate_blocks(1, 0)
    transposed(1, own_half)
    sooner = nq // 2
    for q in range(sooner):
        ecopies[q].wait_recv()
        other_cells(q, own_half)
    from_mate_blocks(1, 1)
    transposed(1, 1 - own_half)
    for q in range(sooner):
        other_cells(q, 1 - own_half)
        other_rows(q)
    for q in range(sooner, nq):
        ecopies[q].wait_recv()
        if q < nq - 1:
            other_cells(q, 0)
            other_cells(q, 1)
            other_rows(q)
        else:
            last[...] = enc[1, q]

    def summed(blocks):
        got = s2buf.at[pl.ds(0, blocks)]
        return rcopy(got, got, b_s, b_r, at_mate)

    @pl.when(mine == 0)
    def _():
        summed(hh - 1).wait_recv()
        total = blk[...]
        for k in range(1, hh):
            total = total + s2buf[k].astype(jnp.float32)
        rcopy(s0buf, s0buf, b_s, c_r, at_mate).wait_recv()
        for k in range(half):
            total = total + s0buf[k].astype(jnp.float32)
        cols_out[...] = (total * scale_c)[:, :d]

    @pl.when(mine != 0)
    def _():
        summed(half - 1).wait_recv()
        total = blk[...]
        for k in froms:
            total = total + s2buf[k].astype(jnp.float32)
        cols_out[...] = (total * scale_c)[:, :d]

    def sent(blocks):
        some = cg.at[0, pl.ds(0, blocks)]
        rcopy(some, some, g_s, gx_r, at_mate).wait_send()

    pl.when(mine == 0)(lambda: sent(2 * near - 1))
    pl.when(mine != 0)(lambda: sent(n - 1))

    @pl.when(mine == 2)
    def _():
        some = gcol.at[pl.ds(0, 3 * (half - near) // 2)]
        rcopy(some, some, w_s, gx_r, at_mate).wait_send()

    def told(blocks):
        some = cg.at[0, pl.ds(0, blocks)]
        rcopy(some, some, m_s, gx_r, at_mate).wait_send()

    pl.when(mine < hh)(lambda: told(n))
    pl.when(mine >= hh)(lambda: told(n - 1))
    def crossed(pieces):
        some = cnt_v.at[pl.ds(0, pieces * gcols * q_w // (2 * LANES))]
        rcopy(some, some, e_s, gx_r, at_x).wait_send()

    pl.when(core == 0)(lambda: crossed(2 * nq))
    pl.when(core == 1)(lambda: crossed(2 * nq + 1))
    some = gcol.at[pl.ds(0, half)]
    rcopy(some, some, a_s, gx_r, at_mate).wait_send()
    pl.when(mine < hh)(lambda: summed(half - 1).wait_send())
    pl.when(mine >= hh)(lambda: summed(half).wait_send())


def scratch_bytes(shapes):
    return sum(math.prod(s.shape) * jnp.dtype(s.dtype).itemsize for s in shapes)


def place(scale_r, rows_in, cols_in, cd1, last, rows_out, cols_out, end, sem):
    d, rows = rows_in.shape
    done = rows - last.shape[1]
    copies = [pltpu.make_async_copy(cols_in, cols_out, sem.at[0]),
              pltpu.make_async_copy(rows_in.at[:, pl.ds(0, done)], rows_out.at[:, pl.ds(0, done)], sem.at[1]),
              pltpu.make_async_copy(end, rows_out.at[:, pl.ds(done, rows - done)], sem.at[2])]
    copies[0].start()
    copies[1].start()
    more = nn(cd1[...], last[...])[:d, :]
    end[...] = (rows_in[:, pl.ds(done, rows - done)] + more) * scale_r
    copies[2].start()
    for cp in copies:
        cp.wait()


def body(row_embed, col_embed, counts, occupancy, row_marg, col_marg, log_total):
    n = lax.axis_size("row")
    d, rows = row_embed.shape
    w = col_embed.shape[2]
    band = counts.shape[2]
    tile = rows // occupancy.shape[0]
    q_w = 2 * tile if rows % (2 * tile) == 0 else tile
    dp = -(-(d + 6) // LANES) * LANES
    half = n // 2
    nq = rows // q_w
    dq = -(-d // 16) * 16
    btiles = band // LANES
    cfg = (n, d, dp, w, band, rows, tile, q_w,
           1.0 / math.sqrt(w * n * lax.axis_size("col")), 1.0 / math.sqrt(rows * n))
    bf, f32 = jnp.bfloat16, jnp.float32
    vm, hb, anywhere = (pl.BlockSpec(memory_space=m) for m in (pltpu.VMEM, pltpu.HBM, pl.ANY))
    dma = lambda *s: pltpu.SemaphoreType.DMA(s) if s else pltpu.SemaphoreType.DMA
    scratch = [
        pltpu.VMEM((d, rows), bf),
        pltpu.VMEM((rows * btiles, LANES), jnp.int32),
        pltpu.VMEM((dp, rows), bf),
        pltpu.VMEM((w, dp), f32),
        pltpu.VMEM((2, n, w, dp), bf),
        pltpu.VMEM((dq, band), bf),
        pltpu.VMEM((2, nq, band, q_w), bf),
        pltpu.VMEM((nq, band, q_w), f32),
        pltpu.VMEM((nq, band, q_w), f32),
        pltpu.VMEM((band, rows), bf),
        pltpu.VMEM((n, w, dp), f32),
        pltpu.VMEM((half, w, dp), f32),
        pltpu.VMEM((half, w, dp), SEND),
        pltpu.VMEM((half, w, dp), SEND),
        pltpu.VMEM((w, d), bf),
        pltpu.VMEM((occupancy.shape[2], occupancy.shape[0]), jnp.int32),
        pltpu.VMEM((1, rows), jnp.int32),
        pltpu.VMEM((1, w), jnp.int32),
        dma(nq + 4),
        dma(), dma(nq), dma(), dma(), dma(2, 2), dma(), dma(2), dma(), dma(2, 2),
        dma(), dma(2), dma(), dma(),
        pltpu.SemaphoreType.REGULAR((half // 2,)),
        pltpu.SemaphoreType.REGULAR,
        dma(), dma(),
        pltpu.VMEM((2, w, dp), bf),
        pltpu.VMEM((half, w, dp), bf),
        pltpu.VMEM((2 * w, rows), bf),
        pltpu.VMEM((band // 2, q_w), bf),
    ]
    limit = min(60 << 20, (6 << 20) + scratch_bytes(scratch[:18]) + 2 * d * rows * 4 + 28 * band * q_w)
    parts = pl.pallas_call(
        functools.partial(kernel, cfg),
        out_shape=(jax.ShapeDtypeStruct((d, rows), f32), jax.ShapeDtypeStruct((w, d), f32),
                   jax.ShapeDtypeStruct((dq, band), bf), jax.ShapeDtypeStruct((band, q_w), bf)),
        in_specs=[hb] * 6 + [pl.BlockSpec(memory_space=pltpu.SMEM)],
        out_specs=(vm,) * 4,
        scratch_shapes=scratch,
        compiler_params=pltpu.CompilerParams(
            collective_id=0, has_side_effects=True, vmem_limit_bytes=limit),
    )(
        *(pltpu.with_memory_space_constraint(x, pltpu.HBM) for x in (
            row_embed,
            jnp.transpose(col_embed, (1, 2, 0)).reshape(w, d),
            counts.reshape(rows * btiles, LANES),
            jnp.transpose(occupancy, (1, 2, 0)).reshape(occupancy.shape[2], occupancy.shape[0]),
            row_marg.reshape(1, rows),
            col_marg,
        )),
        log_total,
    )
    grad_rows, grad_cols = pl.pallas_call(
        functools.partial(place, cfg[8]),
        out_shape=(jax.ShapeDtypeStruct((d, rows), f32), jax.ShapeDtypeStruct((w, d), f32)),
        in_specs=[vm] * 4,
        out_specs=(hb, hb),
        scratch_shapes=[pltpu.VMEM((d, q_w), f32), pltpu.SemaphoreType.DMA((3,))],
        compiler_params=pltpu.CompilerParams(vmem_limit_bytes=limit),
    )(*(pltpu.with_memory_space_constraint(x, pltpu.VMEM) for x in parts))
    return grad_rows, jnp.transpose(grad_cols.reshape(1, w, d), (2, 0, 1))


def solution(mesh):
    placed = (
        P(None, "row"),
        P(None, "col", "row"),
        P("row", "col", None),
        P("row", "col", None),
        P("row"),
        P("col", "row"),
        P(),
    )
    return jax.shard_map(
        body,
        mesh=mesh,
        in_specs=placed,
        out_specs=(P(None, "row"), P(None, "col", "row")),
        check_vma=False,
    )
```
